256 devices in a mesh: side: 2 (over x_hi), row: 32 (over y, z), col: 4 (over x_lo, core).
Axes of the slice: x: 4 (x_hi: 2, x_lo: 2; x = x_hi * 2 + x_lo), y: 4, z: 8, core: 2. Of those that a mesh axis runs over, the one named last changes fastest.
Arguments:
- old_vectors: bfloat16 [2, 32768, 16384], P('side', 'row', 'col'), may hold values from -6 to 6
- reflectors: bfloat16 [2, 2, 32768, 512], P('side', None, 'row', 'col'), may hold values from -0.0625 to 0.0625
- triangles: float32 [2, 2, 512, 512], P('side'), may hold values from -0.25 to 0.25
- pole_sq: float32 [32768], replicated, may hold values from 1 to 65536, as said below
- coupling: float32 [32768], replicated, may hold values from -1 to 1
- deflated: int32 [32768], replicated, may hold values 0 or 1
- pole_order: int32 [32768], replicated, may hold values from 0 to 32767, each once
- anchors: int32 [1024], replicated, may hold values from 0 to 32766, as said below
- root_fraction: float32 [1024], replicated, may hold values from 0.2 to 0.8
Outputs:
- vectors: bfloat16 [2, 1024, 32768], P('side', 'col', 'row')
The draws below stay inside these ranges and needn't reach their ends.
Inputs may be any that keep to these rules, and one draw needn't show every extreme that they name: `pole_sq`: strictly increasing; successive entries differ by 0.5 or more. `anchors`: distinct entries.
All inputs are finite; a program needn't handle non-finite values.
Results may differ from the reference program's by a relative error of at most 0.014.
Values may be sent and summed in bfloat16 or wider, within the bound.
A program may use at most 128 MiB of HBM per device.

```python
import jax
import jax.numpy as jnp
from jax import lax

M = 32768
K = 1024
B = 512
P_SIZE = 2


def draw_pole_sq(key, part):
    pole_gaps = jax.random.uniform(jax.random.fold_in(key, 11), (M,), jnp.float32, 0.5, 2.0)
    return 1.0 + jnp.cumsum(pole_gaps) - pole_gaps[0]


def draw_anchors(key, part):
    interior = jax.random.permutation(jax.random.fold_in(key, 21), M - 3)[:K - 2] + 1
    ends_first = jnp.concatenate([jnp.array([0, M - 2], jnp.int32), interior.astype(jnp.int32)])
    return ends_first[jax.random.permutation(jax.random.fold_in(key, 22), K)]


def plant(entries, stream_key, smallest, high):
    spot = [jax.random.randint(jax.random.fold_in(stream_key, axis), (), 0, length) for axis, length in enumerate(entries.shape)]
    widest = entries.shape.index(max(entries.shape))
    beside = spot[:widest] + [(spot[widest] + 1) % entries.shape[widest]] + spot[widest + 1:]
    return entries.at[tuple(spot)].set(smallest).at[tuple(beside)].set(high)


def levels(rng, extent, shards, low, high):
    factor_of, own = 1.0, jax.random.fold_in(rng, 6)
    for dim, blocks in shards:
        steps = jnp.exp(jax.random.uniform(jax.random.fold_in(own, dim), (blocks,), jnp.float32, low / len(shards), high / len(shards)))
        factor_of = factor_of * jnp.repeat(steps, extent[dim] // blocks).reshape([-1 if axis == dim else 1 for axis in range(len(extent))])
    return factor_of


def gaussian(stream_key, extent, scale, reach, shards=(), kind=jnp.bfloat16):
    entries = scale * jax.random.normal(stream_key, extent, jnp.float32)
    if shards:
        entries = entries * levels(stream_key, extent, shards, -0.22, 0.18)
    return jnp.clip(entries, -reach, reach).astype(kind)


def setup_inputs(seed: int = 0) -> dict:
    splits = jax.random.split(jax.random.key(seed), 10)
    return {
        "old_vectors": gaussian(splits[0], (2, M, M // 2), 1.0, 6.0, ((0, 2), (1, 32), (2, 4))),
        "reflectors": gaussian(splits[1], (2, P_SIZE, M, B), (M // 4) ** -0.5, 0.0625, ((0, 2), (2, 32), (3, 4))),
        "triangles": gaussian(splits[2], (2, P_SIZE, B, B), B ** -0.5, 0.25, ((0, 2),), jnp.float32),
        "pole_sq": draw_pole_sq(jax.random.fold_in(splits[9], 71), 0),
        "coupling": jnp.clip(jax.random.uniform(splits[4], (M,), jnp.float32, -1.0, 1.0), -1.0, 1.0),
        "deflated": plant((jax.random.randint(splits[5], (M,), 0, 4) < 1).astype(jnp.int32), jax.random.fold_in(splits[5], 1), 0, 1),
        "pole_order": jax.random.permutation(splits[6], M).astype(jnp.int32),
        "anchors": draw_anchors(jax.random.fold_in(splits[9], 71), 0),
        "root_fraction": jnp.clip(jax.random.uniform(splits[8], (K,), jnp.float32, 0.2, 0.8), 0.2, 0.8),
    }


def reference(old_vectors, reflectors, triangles, pole_sq, coupling, deflated, pole_order, anchors, root_fraction):
    half_order = old_vectors.shape[2]
    anchor_sq = pole_sq[anchors]
    pole_gap = pole_sq[anchors + 1] - anchor_sq
    dead_triplet = deflated[anchors] == 1
    target = pole_order[anchors]
    live_pole = (1 - deflated).astype(pole_sq.dtype)
    denom = pole_sq[:, None] - anchor_sq[None, :] - root_fraction[None, :] * pole_gap[None, :]
    results = []
    for side_index in range(2):
        weight = jnp.ones_like(pole_sq) if side_index == 0 else jnp.sqrt(pole_sq)
        secular = (live_pole * coupling * weight)[:, None] / denom
        squares = lax.optimization_barrier(jnp.sum(secular * secular, axis=0))
        col_scale = jnp.where(dead_triplet, jnp.ones_like(squares), 1.0 / jnp.sqrt(squares + 1e-06))
        placed = jnp.zeros_like(secular).at[pole_order].set(secular)
        onehot = (jnp.arange(2 * half_order, dtype=jnp.int32)[:, None] == target[None, :]).astype(secular.dtype)
        mixing = jnp.where(dead_triplet[None, :], onehot, placed).astype(jnp.bfloat16)
        upper_part = jnp.dot(old_vectors[side_index, :half_order], mixing[:half_order], preferred_element_type=jnp.float32)
        lower_part = jnp.dot(old_vectors[side_index, half_order:], mixing[half_order:], preferred_element_type=jnp.float32)
        current = jnp.concatenate([upper_part, lower_part], axis=0).T * col_scale[:, None]
        for panel_index in reversed(range(P_SIZE)):
            panel_rows = reflectors[side_index, panel_index]
            current_low = current.astype(jnp.bfloat16)
            projected = jnp.dot(current_low, panel_rows, preferred_element_type=jnp.float32)
            upper_tri = jnp.triu(triangles[side_index, panel_index])
            coefficients = jnp.dot(projected, upper_tri.T, precision=lax.Precision.HIGHEST).astype(jnp.bfloat16)
            current = current - jnp.dot(coefficients, panel_rows.T, preferred_element_type=jnp.float32)
        results.append(current.astype(jnp.bfloat16))
    return jnp.stack(results)
```

```python
import functools

import jax
import jax.numpy as jnp
from jax import lax
from jax.experimental import pallas as pl
from jax.experimental.pallas import tpu as pltpu
from jax.sharding import PartitionSpec as P

LANES = 128
R_TILE = 256
PIECES = 3
F32 = jnp.float32
BF16 = jnp.bfloat16
MESH = pl.DeviceIdType.MESH
NT = (((1,), (1,)), ((), ()))
NN = (((1,), (0,)), ((), ()))


def dot(lhs, rhs, dims):
    return lax.dot_general(lhs, rhs, dims, preferred_element_type=F32)


def split3(value):
    high = value.astype(BF16).astype(F32)
    rest = value - high
    middle = rest.astype(BF16).astype(F32)
    return high, middle, rest - middle


def as_column(row):
    return jnp.broadcast_to(row.astype(F32), (LANES, LANES)).T


def kernel(
    cfg,
    old_hbm, refl_hbm, tri_hbm, pole_ref, coup_ref, defl_ref, order_ref, anchor_ref, frac_ref,
    out_ref,
    old_v, tri_v, v_parts, v_full, u_hi, u_lo, table, col_sq, col_num, asq_s, shift_s, code_s,
    mix, merged, on_send, on_recv, cr_send, cr_recv,
    rs_buf, y_recv, z_buf, z_recv, coef_buf,
    load_sem, v_send, v_recv, on_ssem, on_rsem, cr_ssem, cr_rsem,
    ys_sem, yr_sem, zs_sem, zr_sem, gz_ssem, gz_rsem, gy_ssem, gy_rsem,
):
    n_y, n_z, n_col, triplets, width, rows, n_panels, order_rows, panel = cfg
    own = triplets // n_col
    half_rows = n_y * n_z // 2
    n_hi = width // LANES
    n_rb = rows // R_TILE
    chunk = own // (n_y * n_z)
    blk = panel // n_col

    side = lax.axis_index("side")
    row = lax.axis_index("row")
    col = lax.axis_index("col")
    y, z = row // n_z, row % n_z
    x, core = col // 2, col % 2
    sib = {"col": x * 2 + 1 - core}
    across = {"col": (1 - x) * 2 + core}

    def y_peer(d):
        return lax.rem(y + d, n_y)

    def z_peer(d):
        return lax.rem(z + d, n_z)

    peers = [sib, across]
    peers += [{"row": y_peer(d) * n_z + z} for d in range(1, n_y)]
    peers += [{"row": y * n_z + z_peer(d)} for d in range(1, n_z)]

    barrier = pltpu.get_barrier_semaphore()
    for peer in peers:
        pl.semaphore_signal(barrier, inc=1, device_id=peer, device_id_type=MESH)

    load_old = pltpu.make_async_copy(old_hbm.at[0], old_v, load_sem.at[0])
    load_refl = pltpu.make_async_copy(refl_hbm.at[0], v_parts.at[col], load_sem.at[1])
    load_tri = pltpu.make_async_copy(tri_hbm.at[0], tri_v, load_sem.at[2])
    load_refl.start()
    load_old.start()
    load_tri.start()

    pl.semaphore_wait(barrier, len(peers))

    def remote(src, dst, ssem, rsem, peer):
        return pltpu.make_async_remote_copy(
            src_ref=src, dst_ref=dst, send_sem=ssem, recv_sem=rsem, device_id=peer, device_id_type=MESH
        )

    v_across = remote(refl_hbm.at[0], v_parts.at[col], v_send.at[0], v_recv.at[0], across)
    v_sib = remote(refl_hbm.at[0], v_parts.at[col], v_send.at[1], v_recv.at[1], sib)
    v_across.start()
    v_sib.start()

    first = row // half_rows * (width * n_col) + col * width
    sub_hi = lax.broadcasted_iota(jnp.int32, (n_hi, LANES), 0)
    sub_lo = lax.broadcasted_iota(jnp.int32, (LANES, LANES), 0)

    def scatter(g, acc):
        at = pl.ds(pl.multiple_of(g * 8, 8), 8)
        place = order_ref[at, :] - first
        hi, lo = place >> 7, place & (LANES - 1)
        live = (1 - defl_ref[at, :]).astype(F32) * coup_ref[at, :]
        values = split3(pole_ref[at, :]) + split3(live)
        left, right = [], []
        for r in range(8):
            mask = hi[r : r + 1, :] == sub_hi
            left.append(
                jnp.concatenate([jnp.where(mask, v[r : r + 1, :], 0.0) for v in values], axis=0).astype(BF16)
            )
            right.append(jnp.where(lo[r : r + 1, :] == sub_lo, 1.0, 0.0).astype(BF16))
        return acc + dot(jnp.concatenate(left, axis=1), jnp.concatenate(right, axis=1), NT)

    placed = lax.fori_loop(0, order_rows // 8, scatter, jnp.zeros((2 * PIECES * n_hi, LANES), F32))
    part = [placed[i * n_hi : (i + 1) * n_hi, :] for i in range(2 * PIECES)]
    sq = (part[0] + part[1]) + part[2]
    num = (part[3] + part[4]) + part[5]
    num = num * jnp.where(side == 0, jnp.ones_like(sq), jnp.sqrt(sq))
    for h in range(n_hi):
        lanes = slice(h * LANES, (h + 1) * LANES)
        col_sq[:, lanes] = jnp.broadcast_to(sq[h : h + 1, :], (8, LANES))
        col_num[:, lanes] = jnp.broadcast_to(num[h : h + 1, :], (8, LANES))

    pole = pole_ref[...]
    ahead = pltpu.roll(pole, LANES - 1, 1)
    wrapped = pltpu.roll(ahead, order_rows - 1, 0)
    lane_all = lax.broadcasted_iota(jnp.int32, (order_rows, LANES), 1)
    after = jnp.where(lane_all == LANES - 1, wrapped, ahead)
    order = order_ref[...]
    entries = split3(pole) + split3(after) + (
        (order >> 7).astype(F32), (order & (LANES - 1)).astype(F32), defl_ref[...].astype(F32),
    )
    for i, entry in enumerate(entries):
        table[:, i * LANES : (i + 1) * LANES] = entry.astype(BF16)
    lane_row = lax.broadcasted_iota(jnp.int32, (LANES, LANES), 1)
    lane_table = lax.broadcasted_iota(jnp.int32, (LANES, order_rows), 1)
    dead_mark = 65536.0

    for jb in range(triplets // LANES):
        anchor = as_column(anchor_ref[jb : jb + 1, :]).astype(jnp.int32)
        frac = as_column(frac_ref[jb : jb + 1, :])
        pick_hi = jnp.where((anchor >> 7)[:, :1] == lane_table, 1.0, 0.0).astype(BF16)
        found = dot(pick_hi, table[...], NN)
        f = [found[:, i * LANES : (i + 1) * LANES] for i in range(9)]
        pick_lo = (anchor & (LANES - 1)) == lane_row

        def chosen(value):
            return jnp.sum(jnp.where(pick_lo, value, 0.0), axis=1, keepdims=True)

        a_sq = chosen((f[0] + f[1]) + f[2])
        a_next = chosen((f[3] + f[4]) + f[5])
        target = chosen((f[6] * float(LANES) + f[7]) + f[8] * dead_mark)
        gap = a_next - a_sq
        code = jnp.where(target >= dead_mark, target - dead_mark - first.astype(F32), -dead_mark)
        at = slice(jb * LANES, (jb + 1) * LANES)
        asq_s[at, :] = jnp.broadcast_to(a_sq, (LANES, LANES))
        shift_s[at, :] = frac * gap
        code_s[at, :] = jnp.broadcast_to(code, (LANES, LANES))

    load_old.wait()
    lane_wide = lax.broadcasted_iota(jnp.int32, (8, width), 1).astype(F32)

    def make_mixing(first_triplet):
        def group(g, carry):
            parts = []
            for half in range(2):
                at = pl.ds(pl.multiple_of(first_triplet + g * 16 + half * 8, 8), 8)
                a_sq = jnp.tile(asq_s[at, :], (1, n_hi))
                shift = jnp.tile(shift_s[at, :], (1, n_hi))
                code = jnp.tile(code_s[at, :], (1, n_hi))
                den = (col_sq[...] - a_sq) - shift
                value = col_num[...] / den
                onehot = jnp.where(lane_wide == code, 1.0, 0.0)
                parts.append(jnp.where(code > -dead_mark, onehot, value))
            mix[pl.ds(pl.multiple_of(g * 16, 16), 16), :] = jnp.concatenate(parts, axis=0).astype(BF16)
            return carry

        lax.fori_loop(0, own // 16, group, 0)

    def product(rb):
        return dot(mix[...], old_v[pl.ds(pl.multiple_of(rb * R_TILE, R_TILE), R_TILE), :], NT)

    def on_copy(grp, rb):
        return remote(
            on_send.at[grp, rb], on_recv.at[grp, rb], on_ssem.at[grp, rb], on_rsem.at[grp, rb], sib
        )

    def cr_copy(rb):
        return remote(cr_send.at[rb], cr_recv.at[rb], cr_ssem.at[rb], cr_rsem.at[rb], across)

    v_fwd_at = (1 - x) * 2 + core
    v_fwd = remote(v_parts.at[v_fwd_at], v_parts.at[v_fwd_at], v_send.at[2], v_recv.at[2], sib)

    for grp in range(2):
        chip = 1 - x if grp == 0 else x
        make_mixing((chip * 2 + 1 - core) * own)

        def away(rb, carry):
            on_send[grp, rb] = product(rb).astype(BF16)
            on_copy(grp, rb).start()
            return carry

        lax.fori_loop(0, n_rb, away, 0)
        make_mixing((chip * 2 + core) * own)

        def home(rb, carry):
            value = product(rb)
            on_copy(grp, rb).wait()
            value = value + on_recv[grp, rb].astype(F32)
            if grp == 0:
                cr_send[rb] = value.astype(BF16)
                cr_copy(rb).start()
            else:
                merged[rb] = value
            return carry

        lax.fori_loop(0, n_rb, home, 0)
        if grp == 0:
            v_across.wait()
            v_fwd.start()

    my_rows = order_rows // (n_y * n_z)
    own_at = pl.ds(pl.multiple_of(col * own, LANES if own % LANES == 0 else 8), own)
    a_sq, shift = asq_s[own_at, :], shift_s[own_at, :]

    def square(r, acc):
        at = pl.ds(row * my_rows + r, 1)
        sq_row = pole_ref[at, :]
        weight = jnp.where(side == 0, jnp.ones_like(sq_row), jnp.sqrt(sq_row))
        num_row = (1 - defl_ref[at, :]).astype(F32) * coup_ref[at, :] * weight
        secular = num_row / ((sq_row - a_sq) - shift)
        return acc + secular * secular

    squares = lax.fori_loop(0, my_rows, square, jnp.zeros((own, LANES), F32))
    squares = jnp.sum(squares, axis=1, keepdims=True)
    lane_own = lax.broadcasted_iota(jnp.int32, (own, LANES), 1)

    def in_lanes(value, lane):
        pieces = split3(value)
        wide = jnp.where(lane == 0, pieces[0], 0.0)
        wide = jnp.where(lane == 1, pieces[1], wide)
        return jnp.where(lane == 2, pieces[2], wide)

    square_lanes = in_lanes(squares, lane_own)

    load_tri.wait()
    upper = lax.broadcasted_iota(jnp.int32, (panel, panel), 0) <= lax.broadcasted_iota(jnp.int32, (panel, panel), 1)
    for p in range(n_panels):
        u = jnp.where(upper, tri_v[p], 0.0)
        u_high = u.astype(BF16)
        u_hi[p] = u_high
        u_lo[p] = (u - u_high.astype(F32)).astype(BF16)

    load_refl.wait()
    v_sib.wait()
    v_fwd.wait()
    for p in range(n_panels):
        for c in range(n_col):
            v_full[p, :, c * blk : (c + 1) * blk] = v_parts[c, p]

    def arrive(rb, carry):
        cr_copy(rb).wait()
        merged[rb] = merged[rb] + cr_recv[rb].astype(F32)
        return carry

    lax.fori_loop(0, n_rb, arrive, 0)

    n_chunks = n_y * n_z
    lane_chunk = lax.broadcasted_iota(jnp.int32, (chunk, LANES), 1)

    for step in range(n_panels):
        p = n_panels - 1 - step

        def project(rb, acc):
            v_rows = v_full[p, pl.ds(pl.multiple_of(rb * R_TILE, R_TILE), R_TILE), :]
            return acc + dot(merged[rb].astype(BF16), v_rows, NN)

        proj = lax.fori_loop(0, n_rb, project, jnp.zeros((own, panel), F32))
        wide = jnp.concatenate([proj, square_lanes], axis=1)
        rs_buf[step] = wide.reshape(n_chunks, chunk, panel + LANES).astype(BF16)

        y_copies = [
            remote(
                rs_buf.at[step, pl.ds(y_peer(d) * n_z, n_z)], y_recv.at[step, d - 1],
                ys_sem.at[step, d - 1], yr_sem.at[step, d - 1], {"row": y_peer(d) * n_z + z},
            )
            for d in range(1, n_y)
        ]
        for copy in y_copies:
            copy.start()
        for copy in y_copies:
            copy.wait()
        total = rs_buf[step, pl.ds(y * n_z, n_z)].astype(F32)
        for d in range(1, n_y):
            total = total + y_recv[step, d - 1].astype(F32)
        z_buf[step] = total.astype(BF16)

        z_copies = [
            remote(
                z_buf.at[step, z_peer(d)], z_recv.at[step, d - 1],
                zs_sem.at[step, d - 1], zr_sem.at[step, d - 1], {"row": y * n_z + z_peer(d)},
            )
            for d in range(1, n_z)
        ]
        for copy in z_copies:
            copy.start()
        for copy in z_copies:
            copy.wait()
        total = z_buf[step, z].astype(F32)
        for d in range(1, n_z):
            total = total + z_recv[step, d - 1].astype(F32)

        proj_all = total[:, :panel]
        proj_hi = proj_all.astype(BF16).astype(F32)
        stacked = jnp.concatenate([proj_hi, proj_all - proj_hi], axis=0).astype(BF16)
        by_hi = dot(stacked, u_hi[p], NT)
        by_lo = dot(stacked, u_lo[p], NT)
        coef = by_hi[:chunk] + (by_hi[chunk:] + by_lo[:chunk])
        square_sum = jnp.sum(total[:, panel:], axis=1, keepdims=True)
        code = code_s[pl.ds(pl.multiple_of(col * own + row * chunk, 8), chunk), :1]
        scale = jnp.where(code > -dead_mark, 1.0, 1.0 / jnp.sqrt(square_sum + 1e-6))
        coef_buf[step, row] = jnp.concatenate([coef, in_lanes(scale, lane_chunk)], axis=1).astype(BF16)

        gz_copies = [
            remote(
                coef_buf.at[step, row], coef_buf.at[step, row],
                gz_ssem.at[step, d - 1], gz_rsem.at[step, d - 1], {"row": y * n_z + z_peer(d)},
            )
            for d in range(1, n_z)
        ]
        for copy in gz_copies:
            copy.start()
        for copy in gz_copies:
            copy.wait()
        gy_copies = [
            remote(
                coef_buf.at[step, pl.ds(y * n_z, n_z)], coef_buf.at[step, pl.ds(y * n_z, n_z)],
                gy_ssem.at[step, d - 1], gy_rsem.at[step, d - 1], {"row": y_peer(d) * n_z + z},
            )
            for d in range(1, n_y)
        ]
        for copy in gy_copies:
            copy.start()
        for copy in gy_copies:
            copy.wait()

        gathered = coef_buf[step].astype(F32).reshape(own, panel + LANES)
        coef_all = gathered[:, :panel].astype(BF16)
        last = step == n_panels - 1
        scale_all = jnp.sum(gathered[:, panel:], axis=1, keepdims=True)

        for rb in range(n_rb):
            at = slice(rb * R_TILE, (rb + 1) * R_TILE)
            value = merged[rb] - dot(coef_all, v_full[p, at, :], NT)
            if last:
                out_ref[0, :, at] = (value * scale_all).astype(BF16)
            else:
                merged[rb] = value


def per_device(cfg, old_vectors, reflectors, triangles, pole_sq, coupling, deflated, pole_order, anchors, root_fraction):
    n_y, n_z, n_col, triplets, width, rows, n_panels, order_rows, panel = cfg
    own = triplets // n_col
    n_rb = rows // R_TILE
    chunk = own // (n_y * n_z)
    lane_rows = lambda a: a.reshape(-1, LANES)
    dma, vmem = pltpu.SemaphoreType.DMA, pltpu.VMEM
    wide = panel + LANES
    scratch = [
        vmem((rows, width), BF16),
        vmem((n_panels, panel, panel), F32),
        vmem((n_col, n_panels, rows, panel // n_col), BF16),
        vmem((n_panels, rows, panel), BF16),
        vmem((n_panels, panel, panel), BF16),
        vmem((n_panels, panel, panel), BF16),
        vmem((order_rows, 9 * LANES), BF16),
        vmem((8, width), F32),
        vmem((8, width), F32),
        vmem((triplets, LANES), F32),
        vmem((triplets, LANES), F32),
        vmem((triplets, LANES), F32),
        vmem((own, width), BF16),
        vmem((n_rb, own, R_TILE), F32),
        vmem((2, n_rb, own, R_TILE), BF16),
        vmem((2, n_rb, own, R_TILE), BF16),
        vmem((n_rb, own, R_TILE), BF16),
        vmem((n_rb, own, R_TILE), BF16),
        vmem((n_panels, n_y * n_z, chunk, wide), BF16),
        vmem((n_panels, n_y - 1, n_z, chunk, wide), BF16),
        vmem((n_panels, n_z, chunk, wide), BF16),
        vmem((n_panels, n_z - 1, chunk, wide), BF16),
        vmem((n_panels, n_y * n_z, chunk, wide), BF16),
        dma((3,)), dma((3,)), dma((3,)),
        dma((2, n_rb)), dma((2, n_rb)), dma((n_rb,)), dma((n_rb,)),
        dma((n_panels, n_y - 1)), dma((n_panels, n_y - 1)),
        dma((n_panels, n_z - 1)), dma((n_panels, n_z - 1)),
        dma((n_panels, n_z - 1)), dma((n_panels, n_z - 1)),
        dma((n_panels, n_y - 1)), dma((n_panels, n_y - 1)),
    ]
    any_spec, vmem_spec = pl.BlockSpec(memory_space=pl.ANY), pl.BlockSpec(memory_space=pltpu.VMEM)
    return pl.pallas_call(
        functools.partial(kernel, cfg),
        out_shape=jax.ShapeDtypeStruct((1, own, rows), BF16),
        in_specs=[any_spec] * 3 + [vmem_spec] * 6,
        out_specs=vmem_spec,
        scratch_shapes=scratch,
        compiler_params=pltpu.CompilerParams(
            collective_id=0, has_side_effects=True, vmem_limit_bytes=56 << 20
        ),
    )(
        old_vectors, reflectors, triangles,
        lane_rows(pole_sq), lane_rows(coupling), lane_rows(deflated), lane_rows(pole_order),
        lane_rows(anchors), lane_rows(root_fraction),
    )


def solution(mesh):
    n_row, n_col = mesh.shape["row"], mesh.shape["col"]
    n_y = 4
    n_z = n_row // n_y

    def whole(old_vectors, reflectors, triangles, pole_sq, coupling, deflated, pole_order, anchors, root_fraction):
        size, panel = reflectors.shape[2:]
        cfg = (
            n_y, n_z, n_col, anchors.shape[0], old_vectors.shape[2] // n_col, size // n_row,
            reflectors.shape[1], size // LANES, panel,
        )
        in_specs = (P("side", "row", "col"), P("side", None, "row", "col"), P("side", None, None, None)) + (P(),) * 6
        return jax.shard_map(
            functools.partial(per_device, cfg), mesh=mesh, in_specs=in_specs,
            out_specs=P("side", "col", "row"), check_vma=False,
        )(old_vectors, reflectors, triangles, pole_sq, coupling, deflated, pole_order, anchors, root_fraction)

    return whole
```

```python
import functools

import jax
import jax.numpy as jnp
from jax import lax
from jax.experimental import pallas as pl
from jax.experimental.pallas import tpu as pltpu
from jax.sharding import PartitionSpec as P

LANES = 128
R_TILE = 256
PIECES = 3
F32 = jnp.float32
BF16 = jnp.bfloat16
MESH = pl.DeviceIdType.MESH
NT = (((1,), (1,)), ((), ()))
NN = (((1,), (0,)), ((), ()))
TN = (((0,), (0,)), ((), ()))


def dot(lhs, rhs, dims):
    return lax.dot_general(lhs, rhs, dims, preferred_element_type=F32)


def split3(value):
    high = value.astype(BF16).astype(F32)
    rest = value - high
    middle = rest.astype(BF16).astype(F32)
    return high, middle, rest - middle


def as_column(row):
    return jnp.broadcast_to(row.astype(F32), (LANES, LANES)).T


def kernel(
    cfg,
    old_hbm, refl_hbm, tri_hbm, pole_ref, coup_ref, defl_ref, order_ref, anchor_ref, frac_ref,
    out_ref,
    old_v, tri_v, v_parts, v_full, u_hi, u_lo, table, col_sq, col_num, asq_s, shift_s, code_s, scale_s,
    mix, hold, merged, proj_acc, on_send, on_recv, cr_send, cr_recv, gram_all,
    sq_own, sq_y, sq_sum, sq_z,
    p_buf, p_y, p_z, p_zr, p_all, g_buf, g_y, g_z, g_zr, g_all,
    load_sem, v_send, v_recv, on_ssem, on_rsem, cr_ssem, cr_rsem, gram_ssem, gram_rsem,
    sy_ssem, sy_rsem, sz_ssem, sz_rsem,
    ys_sem, yr_sem, zs_sem, zr_sem, gz_ssem, gz_rsem, gy_ssem, gy_rsem,
):
    n_y, n_z, n_col, triplets, width, rows, n_panels, order_rows, panel = cfg
    own = triplets // n_col
    half_rows = n_y * n_z // 2
    n_chunks = n_y * n_z
    n_hi = width // LANES
    n_rb = rows // R_TILE
    chunk = own // n_chunks
    blk = panel // n_col
    half_panel = panel // 2
    g_chunk = half_panel // n_chunks
    scatter_rows = min(64, order_rows)

    side = lax.axis_index("side")
    row = lax.axis_index("row")
    col = lax.axis_index("col")
    y, z = row // n_z, row % n_z
    x, core = col // 2, col % 2
    sib = {"col": x * 2 + 1 - core}
    across = {"col": (1 - x) * 2 + core}

    def y_peer(d):
        return lax.rem(y + d, n_y)

    def z_peer(d):
        return lax.rem(z + d, n_z)

    def y_dev(d):
        return {"row": y_peer(d) * n_z + z}

    def z_dev(d):
        return {"row": y * n_z + z_peer(d)}

    peers = [sib, across] + [y_dev(d) for d in range(1, n_y)] + [z_dev(d) for d in range(1, n_z)]
    barrier = pltpu.get_barrier_semaphore()
    for peer in peers:
        pl.semaphore_signal(barrier, inc=1, device_id=peer, device_id_type=MESH)

    load_refl = pltpu.make_async_copy(refl_hbm.at[0], v_parts.at[col], load_sem.at[1])
    load_old = pltpu.make_async_copy(old_hbm.at[0], old_v, load_sem.at[0])
    load_tri = pltpu.make_async_copy(tri_hbm.at[0], tri_v, load_sem.at[2])
    load_refl.start()
    load_old.start()
    load_tri.start()

    def remote(src, dst, ssem, rsem, peer):
        return pltpu.make_async_remote_copy(
            src_ref=src, dst_ref=dst, send_sem=ssem, recv_sem=rsem, device_id=peer, device_id_type=MESH
        )

    first = row // half_rows * (width * n_col) + col * width
    sub_hi = lax.broadcasted_iota(jnp.int32, (n_hi, LANES), 0)
    sub_lo = lax.broadcasted_iota(jnp.int32, (LANES, LANES), 0)

    def scatter(g, acc):
        left, right = [], []
        for b in range(scatter_rows // 8):
            at = pl.ds(pl.multiple_of(g * scatter_rows + b * 8, 8), 8)
            place = order_ref[at, :] - first
            hi, lo = place >> 7, place & (LANES - 1)
            live = (1 - defl_ref[at, :]).astype(F32) * coup_ref[at, :]
            values = split3(pole_ref[at, :]) + split3(live)
            for r in range(8):
                mask = hi[r : r + 1, :] == sub_hi
                left.append(
                    jnp.concatenate([jnp.where(mask, v[r : r + 1, :], 0.0) for v in values], axis=0).astype(BF16)
                )
                right.append(jnp.where(lo[r : r + 1, :] == sub_lo, 1.0, 0.0).astype(BF16))
        return acc + dot(jnp.concatenate(left, axis=1), jnp.concatenate(right, axis=1), NT)

    placed = lax.fori_loop(
        0, order_rows // scatter_rows, scatter, jnp.zeros((2 * PIECES * n_hi, LANES), F32)
    )
    part = [placed[i * n_hi : (i + 1) * n_hi, :] for i in range(2 * PIECES)]
    sq = (part[0] + part[1]) + part[2]
    num = (part[3] + part[4]) + part[5]
    num = num * jnp.where(side == 0, jnp.ones_like(sq), jnp.sqrt(sq))
    for h in range(n_hi):
        lanes = slice(h * LANES, (h + 1) * LANES)
        col_sq[:, lanes] = jnp.broadcast_to(sq[h : h + 1, :], (8, LANES))
        col_num[:, lanes] = jnp.broadcast_to(num[h : h + 1, :], (8, LANES))

    pl.semaphore_wait(barrier, len(peers))

    v_across = remote(refl_hbm.at[0], v_parts.at[col], v_send.at[0], v_recv.at[0], across)
    v_sib = remote(refl_hbm.at[0], v_parts.at[col], v_send.at[1], v_recv.at[1], sib)
    v_across.start()
    v_sib.start()
    v_fwd_at = (1 - x) * 2 + core
    v_fwd = remote(v_parts.at[v_fwd_at], v_parts.at[v_fwd_at], v_send.at[2], v_recv.at[2], sib)

    pole = pole_ref[...]
    ahead = pltpu.roll(pole, LANES - 1, 1)
    wrapped = pltpu.roll(ahead, order_rows - 1, 0)
    lane_all = lax.broadcasted_iota(jnp.int32, (order_rows, LANES), 1)
    after = jnp.where(lane_all == LANES - 1, wrapped, ahead)
    order = order_ref[...]
    entries = split3(pole) + split3(after) + (
        (order >> 7).astype(F32), (order & (LANES - 1)).astype(F32), defl_ref[...].astype(F32),
    )
    for i, entry in enumerate(entries):
        table[:, i * LANES : (i + 1) * LANES] = entry.astype(BF16)
    lane_row = lax.broadcasted_iota(jnp.int32, (LANES, LANES), 1)
    lane_table = lax.broadcasted_iota(jnp.int32, (LANES, order_rows), 1)
    dead_mark = 65536.0

    for jb in range(triplets // LANES):
        anchor = as_column(anchor_ref[jb : jb + 1, :]).astype(jnp.int32)
        frac = as_column(frac_ref[jb : jb + 1, :])
        pick_hi = jnp.where((anchor >> 7)[:, :1] == lane_table, 1.0, 0.0).astype(BF16)
        found = dot(pick_hi, table[...], NN)
        f = [found[:, i * LANES : (i + 1) * LANES] for i in range(9)]
        pick_lo = (anchor & (LANES - 1)) == lane_row

        def chosen(value):
            return jnp.sum(jnp.where(pick_lo, value, 0.0), axis=1, keepdims=True)

        a_sq = chosen((f[0] + f[1]) + f[2])
        a_next = chosen((f[3] + f[4]) + f[5])
        target = chosen((f[6] * float(LANES) + f[7]) + f[8] * dead_mark)
        gap = a_next - a_sq
        code = jnp.where(target >= dead_mark, target - dead_mark - first.astype(F32), -dead_mark)
        at = slice(jb * LANES, (jb + 1) * LANES)
        asq_s[at, :] = jnp.broadcast_to(a_sq, (LANES, LANES))
        shift_s[at, :] = frac * gap
        code_s[at, :] = jnp.broadcast_to(code, (LANES, LANES))

    my_rows = order_rows // n_chunks
    own_at = pl.ds(pl.multiple_of(col * own, LANES), own)
    own_sq, own_shift = asq_s[own_at, :], shift_s[own_at, :]
    squares = jnp.zeros((own, LANES), F32)
    for r in range(my_rows):
        at = pl.ds(row * my_rows + r, 1)
        sq_row = pole_ref[at, :]
        weight = jnp.where(side == 0, jnp.ones_like(sq_row), jnp.sqrt(sq_row))
        num_row = (1 - defl_ref[at, :]).astype(F32) * coup_ref[at, :] * weight
        secular = num_row / ((sq_row - own_sq) - own_shift)
        squares = squares + secular * secular
    sq_own[...] = jnp.zeros((8, LANES), F32)
    for h in range(own // LANES):
        column = jnp.sum(squares[h * LANES : (h + 1) * LANES, :], axis=1, keepdims=True)
        sq_own[h : h + 1, :] = jnp.broadcast_to(column, (LANES, LANES)).T[:1, :]
    sy_copies = [
        remote(sq_own, sq_y.at[d - 1], sy_ssem.at[d - 1], sy_rsem.at[d - 1], y_dev(d)) for d in range(1, n_y)
    ]
    sz_copies = [
        remote(sq_sum, sq_z.at[d - 1], sz_ssem.at[d - 1], sz_rsem.at[d - 1], z_dev(d)) for d in range(1, n_z)
    ]
    for copy in sy_copies:
        copy.start()

    lane_wide = lax.broadcasted_iota(jnp.int32, (8, width), 1).astype(F32)

    def make_mixing(grp, g):
        chip = 1 - x if grp == 0 else x
        base = jnp.where(g < own // 16, (chip * 2 + 1 - core) * own, (chip * 2 + core) * own - own)
        parts = []
        for half in range(2):
            at = pl.ds(pl.multiple_of(base + g * 16 + half * 8, 8), 8)
            a_sq = jnp.tile(asq_s[at, :], (1, n_hi))
            shift = jnp.tile(shift_s[at, :], (1, n_hi))
            code = jnp.tile(code_s[at, :], (1, n_hi))
            den = (col_sq[...] - a_sq) - shift
            value = col_num[...] / den
            onehot = jnp.where(lane_wide == code, 1.0, 0.0)
            parts.append(jnp.where(code > -dead_mark, onehot, value))
        mix[grp, pl.ds(pl.multiple_of(g * 16, 16), 16), :] = jnp.concatenate(parts, axis=0).astype(BF16)

    def first_mixing(g, carry):
        make_mixing(0, g)
        return carry

    lax.fori_loop(0, own // 8, first_mixing, 0)
    load_old.wait()

    def product(grp, rb):
        return dot(mix[grp], old_v[pl.ds(pl.multiple_of(rb * R_TILE, R_TILE), R_TILE), :], NT)

    def on_copy(grp, rb):
        return remote(
            on_send.at[grp, rb], on_recv.at[grp, rb], on_ssem.at[grp, rb], on_rsem.at[grp, rb], sib
        )

    def cr_copy(rb):
        return remote(cr_send.at[rb], cr_recv.at[rb], cr_ssem.at[rb], cr_rsem.at[rb], across)

    def pass_across(rb):
        on_copy(0, rb).wait()
        cr_send[rb] = (hold[rb] + on_recv[0, rb].astype(F32)).astype(BF16)
        cr_copy(rb).start()

    per_rb = own // 8 // n_rb

    def other_chip(rb, carry):
        value = product(0, rb)
        for q in range(per_rb):
            make_mixing(1, rb * per_rb + q)
        on_send[0, rb] = value[:own].astype(BF16)
        on_copy(0, rb).start()
        hold[rb] = value[own:]

        @pl.when(rb > 0)
        def _():
            pass_across(rb - 1)

        return carry

    lax.fori_loop(0, n_rb, other_chip, 0)
    pass_across(n_rb - 1)

    for copy in sy_copies:
        copy.wait()
    total = sq_own[...]
    for d in range(1, n_y):
        total = total + sq_y[d - 1]
    sq_sum[...] = total
    for copy in sz_copies:
        copy.start()

    v_across.wait()
    v_fwd.start()

    def own_chip(rb, carry):
        value = product(1, rb)
        on_send[1, rb] = value[:own].astype(BF16)
        on_copy(1, rb).start()
        merged[rb] = value[own:]
        return carry

    lax.fori_loop(0, n_rb // 2, own_chip, 0)

    def reduction(i, buf, from_y, z_in, from_z, everything):
        y_out = [
            remote(buf.at[pl.ds(y_peer(d) * n_z, n_z)], from_y.at[d - 1], ys_sem.at[i, d - 1], yr_sem.at[i, d - 1], y_dev(d))
            for d in range(1, n_y)
        ]
        z_out = [
            remote(z_in.at[z_peer(d)], from_z.at[d - 1], zs_sem.at[i, d - 1], zr_sem.at[i, d - 1], z_dev(d))
            for d in range(1, n_z)
        ]
        mine = everything.at[row]
        z_back = [remote(mine, mine, gz_ssem.at[i, d - 1], gz_rsem.at[i, d - 1], z_dev(d)) for d in range(1, n_z)]
        line = everything.at[pl.ds(y * n_z, n_z)]
        y_back = [remote(line, line, gy_ssem.at[i, d - 1], gy_rsem.at[i, d - 1], y_dev(d)) for d in range(1, n_y)]

        def start(copies):
            for copy in copies:
                copy.start()

        def wait(copies):
            for copy in copies:
                copy.wait()

        def y_to_z():
            wait(y_out)
            summed = buf[pl.ds(y * n_z, n_z)].astype(F32)
            for d in range(1, n_y):
                summed = summed + from_y[d - 1].astype(F32)
            z_in[...] = summed.astype(BF16)
            start(z_out)

        def finish():
            wait(z_out)
            summed = z_in[z].astype(F32)
            for d in range(1, n_z):
                summed = summed + from_z[d - 1].astype(F32)
            return summed

        def send_back(value):
            everything[row] = value
            start(z_back)

        def z_to_y_back():
            wait(z_back)
            start(y_back)

        return (lambda: start(y_out)), y_to_z, finish, send_back, z_to_y_back, (lambda: wait(y_back))

    red_proj = [
        reduction(i, p_buf.at[i], p_y.at[i], p_z.at[i], p_zr.at[i], p_all.at[i]) for i in range(2)
    ]
    red_gram = reduction(2, g_buf, g_y, g_z, g_zr, g_all)

    load_refl.wait()
    v_sib.wait()
    v_fwd.wait()
    for p in range(n_panels):
        for c in range(n_col):
            v_full[p, :, c * blk : (c + 1) * blk] = v_parts[c, p]
    half_at = pl.ds(pl.multiple_of(core * half_panel, half_panel), half_panel)
    gram = dot(v_full[1, :, half_at], v_full[0], TN)
    g_buf[...] = gram.reshape(n_chunks, g_chunk, panel).astype(BF16)
    red_gram[0]()

    lax.fori_loop(n_rb // 2, n_rb, own_chip, 0)

    load_tri.wait()
    upper = lax.broadcasted_iota(jnp.int32, (panel, panel), 0) <= lax.broadcasted_iota(jnp.int32, (panel, panel), 1)
    for p in range(n_panels):
        u = jnp.where(upper, tri_v[p], 0.0)
        u_high = u.astype(BF16)
        u_hi[p] = u_high
        u_lo[p] = (u - u_high.astype(F32)).astype(BF16)
    red_gram[1]()

    for copy in sz_copies:
        copy.wait()
    total = sq_sum[...]
    for d in range(1, n_z):
        total = total + sq_z[d - 1]
    for h in range(own // LANES):
        scale = 1.0 / jnp.sqrt(as_column(total[h : h + 1, :]) + 1e-6)
        at = pl.ds(pl.multiple_of(col * own + h * LANES, LANES), LANES)
        scale_s[h * LANES : (h + 1) * LANES, :] = jnp.where(code_s[at, :] > -dead_mark, 1.0, scale)

    for rb in range(n_rb):
        at = slice(rb * R_TILE, (rb + 1) * R_TILE)
        on_copy(1, rb).wait()
        cr_copy(rb).wait()
        value = merged[rb] + on_recv[1, rb].astype(F32) + cr_recv[rb].astype(F32)
        merged[rb] = value
        value_low = value.astype(BF16)
        if rb < n_rb - 1:
            for p in range(2):
                term = dot(value_low, v_full[p, at, :], NN)
                proj_acc[p] = term if rb == 0 else proj_acc[p] + term
    for i in range(2):
        p = 1 - i
        term = proj_acc[p] + dot(value_low, v_full[p, at, :], NN)
        p_buf[i] = term.reshape(n_chunks, chunk, panel).astype(BF16)
        red_proj[i][0]()

    red_gram[3](red_gram[2]().astype(BF16))
    red_proj[0][1]()
    red_proj[1][1]()
    red_gram[4]()

    def apply_triangle(value, p):
        high = value.astype(BF16).astype(F32)
        stacked = jnp.concatenate([high, value - high], axis=0).astype(BF16)
        by_hi = dot(stacked, u_hi[p], NT)
        by_lo = dot(stacked, u_lo[p], NT)
        return (by_hi[:chunk] + (by_hi[chunk:] + by_lo[:chunk])).astype(BF16)

    coef_1 = apply_triangle(red_proj[0][2](), 1)
    red_proj[0][3](coef_1)
    red_gram[5]()
    gram_copy = remote(g_all, gram_all.at[core], gram_ssem, gram_rsem, sib)
    gram_copy.start()
    gram_all[core] = g_all[...]
    proj_0 = red_proj[1][2]()
    gram_copy.wait()
    gram_rows = gram_all[...].astype(F32).reshape(panel, panel).astype(BF16)
    coef_0 = apply_triangle(proj_0 - dot(coef_1, gram_rows, NN), 0)
    red_proj[1][3](coef_0)
    red_proj[0][4]()
    red_proj[1][4]()

    for i in range(2):
        p = 1 - i
        red_proj[i][5]()
        coef_all = p_all[i].astype(F32).reshape(own, panel).astype(BF16)
        for rb in range(n_rb):
            at = slice(rb * R_TILE, (rb + 1) * R_TILE)
            value = merged[rb] - dot(coef_all, v_full[p, at, :], NT)
            if i == 1:
                out_ref[0, :, at] = (value * jnp.tile(scale_s[...], (1, R_TILE // LANES))).astype(BF16)
            else:
                merged[rb] = value


def per_device(cfg, old_vectors, reflectors, triangles, pole_sq, coupling, deflated, pole_order, anchors, root_fraction):
    n_y, n_z, n_col, triplets, width, rows, n_panels, order_rows, panel = cfg
    own = triplets // n_col
    n_rb = rows // R_TILE
    chunk = own // (n_y * n_z)
    lane_rows = lambda a: a.reshape(-1, LANES)
    dma, vmem = pltpu.SemaphoreType.DMA, pltpu.VMEM
    n_row, half = n_y * n_z, panel // 2
    scratch = [
        vmem((rows, width), BF16),
        vmem((n_panels, panel, panel), F32),
        vmem((n_col, n_panels, rows, panel // n_col), BF16),
        vmem((n_panels, rows, panel), BF16),
        vmem((n_panels, panel, panel), BF16),
        vmem((n_panels, panel, panel), BF16),
        vmem((order_rows, 9 * LANES), BF16),
        vmem((8, width), F32),
        vmem((8, width), F32),
        vmem((triplets, LANES), F32),
        vmem((triplets, LANES), F32),
        vmem((triplets, LANES), F32),
        vmem((own, LANES), F32),
        vmem((2, 2 * own, width), BF16),
        vmem((n_rb, own, R_TILE), F32),
        vmem((n_rb, own, R_TILE), F32),
        vmem((2, own, panel), F32),
        vmem((2, n_rb, own, R_TILE), BF16),
        vmem((2, n_rb, own, R_TILE), BF16),
        vmem((n_rb, own, R_TILE), BF16),
        vmem((n_rb, own, R_TILE), BF16),
        vmem((2, n_row, half // n_row, panel), BF16),
        vmem((8, LANES), F32), vmem((n_y - 1, 8, LANES), F32),
        vmem((8, LANES), F32), vmem((n_z - 1, 8, LANES), F32),
        vmem((2, n_row, chunk, panel), BF16),
        vmem((2, n_y - 1, n_z, chunk, panel), BF16),
        vmem((2, n_z, chunk, panel), BF16),
        vmem((2, n_z - 1, chunk, panel), BF16),
        vmem((2, n_row, chunk, panel), BF16),
        vmem((n_row, half // n_row, panel), BF16),
        vmem((n_y - 1, n_z, half // n_row, panel), BF16),
        vmem((n_z, half // n_row, panel), BF16),
        vmem((n_z - 1, half // n_row, panel), BF16),
        vmem((n_row, half // n_row, panel), BF16),
        dma((3,)), dma((3,)), dma((3,)),
        dma((2, n_rb)), dma((2, n_rb)), dma((n_rb,)), dma((n_rb,)), dma, dma,
        dma((n_y - 1,)), dma((n_y - 1,)), dma((n_z - 1,)), dma((n_z - 1,)),
        dma((3, n_y - 1)), dma((3, n_y - 1)),
        dma((3, n_z - 1)), dma((3, n_z - 1)),
        dma((3, n_z - 1)), dma((3, n_z - 1)),
        dma((3, n_y - 1)), dma((3, n_y - 1)),
    ]
    any_spec, vmem_spec = pl.BlockSpec(memory_space=pl.ANY), pl.BlockSpec(memory_space=pltpu.VMEM)
    return pl.pallas_call(
        functools.partial(kernel, cfg),
        out_shape=jax.ShapeDtypeStruct((1, own, rows), BF16),
        in_specs=[any_spec] * 3 + [vmem_spec] * 6,
        out_specs=vmem_spec,
        scratch_shapes=scratch,
        compiler_params=pltpu.CompilerParams(
            collective_id=0, has_side_effects=True, vmem_limit_bytes=56 << 20
        ),
    )(
        old_vectors, reflectors, triangles,
        lane_rows(pole_sq), lane_rows(coupling), lane_rows(deflated), lane_rows(pole_order),
        lane_rows(anchors), lane_rows(root_fraction),
    )


def solution(mesh):
    n_row, n_col = mesh.shape["row"], mesh.shape["col"]
    n_y = 4
    n_z = n_row // n_y

    def whole(old_vectors, reflectors, triangles, pole_sq, coupling, deflated, pole_order, anchors, root_fraction):
        size, panel = reflectors.shape[2:]
        cfg = (
            n_y, n_z, n_col, anchors.shape[0], old_vectors.shape[2] // n_col, size // n_row,
            reflectors.shape[1], size // LANES, panel,
        )
        in_specs = (P("side", "row", "col"), P("side", None, "row", "col"), P("side", None, None, None)) + (P(),) * 6
        return jax.shard_map(
            functools.partial(per_device, cfg), mesh=mesh, in_specs=in_specs,
            out_specs=P("side", "col", "row"), check_vma=False,
        )(old_vectors, reflectors, triangles, pole_sq, coupling, deflated, pole_order, anchors, root_fraction)

    return whole
```

```python
import functools

import jax
import jax.numpy as jnp
from jax import lax
from jax.experimental import pallas as pl
from jax.experimental.pallas import tpu as pltpu
from jax.sharding import PartitionSpec as P

LANES = 128
R_TILE = 256
PIECES = 3
F32 = jnp.float32
BF16 = jnp.bfloat16
MESH = pl.DeviceIdType.MESH
NT = (((1,), (1,)), ((), ()))
NN = (((1,), (0,)), ((), ()))
TN = (((0,), (0,)), ((), ()))


def dot(lhs, rhs, dims):
    return lax.dot_general(lhs, rhs, dims, preferred_element_type=F32)


def split3(value):
    high = value.astype(BF16).astype(F32)
    rest = value - high
    middle = rest.astype(BF16).astype(F32)
    return high, middle, rest - middle


def as_column(row):
    return jnp.broadcast_to(row.astype(F32), (LANES, LANES)).T


def kernel(
    cfg,
    old_hbm, refl_hbm, tri_hbm, pole_ref, coup_ref, defl_ref, order_ref, anchor_ref, frac_ref,
    out_ref,
    old_v, tri_v, v_parts, v_full, u_hi, u_lo, table, col_sq, col_num, asq_s, shift_s, code_s, scale_s,
    mix, hold, merged, proj_acc, on_send, on_recv, cr_send, cr_recv, gram_all,
    sq_own, sq_y, sq_sum, sq_z,
    p_buf, p_y, p_z, p_zr, p_all, g_buf, g_y, g_z, g_zr, g_all,
    load_sem, v_send, v_recv, on_ssem, on_rsem, cr_ssem, cr_rsem, gram_ssem, gram_rsem,
    sy_ssem, sy_rsem, sz_ssem, sz_rsem,
    ys_sem, yr_sem, zs_sem, zr_sem, gz_ssem, gz_rsem, gy_ssem, gy_rsem, meet_sem,
):
    n_y, n_z, n_col, triplets, width, rows, n_panels, order_rows, panel = cfg
    own = triplets // n_col
    half_rows = n_y * n_z // 2
    n_chunks = n_y * n_z
    n_hi = width // LANES
    n_rb = rows // R_TILE
    chunk = own // n_chunks
    blk = panel // n_col
    half_panel = panel // 2
    g_chunk = half_panel // n_chunks
    scatter_rows = min(128, order_rows)

    side = lax.axis_index("side")
    row = lax.axis_index("row")
    col = lax.axis_index("col")
    y, z = row // n_z, row % n_z
    x, core = col // 2, col % 2
    sib = {"col": x * 2 + 1 - core}
    across = {"col": (1 - x) * 2 + core}

    def y_peer(d):
        return lax.rem(y + d, n_y)

    def z_peer(d):
        return lax.rem(z + d, n_z)

    def y_dev(d):
        return {"row": y_peer(d) * n_z + z}

    def z_dev(d):
        return {"row": y * n_z + z_peer(d)}

    y_near = sorted({1, n_y - 1})
    z_near = sorted({1, n_z - 1})
    z_mid = sorted({d % n_z for d in (1, -1, 2, -2)} - {0})
    near = [y_dev(d) for d in y_near] + [z_dev(d) for d in z_near]
    middle = [z_dev(d) for d in z_mid]
    peers = [sib, across] + near
    barrier = pltpu.get_barrier_semaphore()
    for peer in peers:
        pl.semaphore_signal(barrier, inc=1, device_id=peer, device_id_type=MESH)

    load_refl = pltpu.make_async_copy(refl_hbm.at[0], v_parts.at[col], load_sem.at[1])
    load_old = pltpu.make_async_copy(old_hbm.at[0], old_v, load_sem.at[0])
    load_tri = pltpu.make_async_copy(tri_hbm.at[0], tri_v, load_sem.at[2])
    load_refl.start()
    load_old.start()
    load_tri.start()

    def remote(src, dst, ssem, rsem, peer):
        return pltpu.make_async_remote_copy(
            src_ref=src, dst_ref=dst, send_sem=ssem, recv_sem=rsem, device_id=peer, device_id_type=MESH
        )

    pl.semaphore_wait(barrier, len(peers))
    for peer in near:
        pl.semaphore_signal(meet_sem.at[0], inc=1, device_id=peer, device_id_type=MESH)

    v_across = remote(refl_hbm.at[0], v_parts.at[col], v_send.at[0], v_recv.at[0], across)
    v_sib = remote(refl_hbm.at[0], v_parts.at[col], v_send.at[1], v_recv.at[1], sib)
    v_across.start()
    v_sib.start()
    v_fwd_at = (1 - x) * 2 + core
    v_fwd = remote(v_parts.at[v_fwd_at], v_parts.at[v_fwd_at], v_send.at[2], v_recv.at[2], sib)

    first = row // half_rows * (width * n_col) + col * width
    sub_hi = lax.broadcasted_iota(jnp.int32, (n_hi, LANES), 0)
    sub_lo = lax.broadcasted_iota(jnp.int32, (LANES, LANES), 0)

    def scatter(g, acc):
        left, right = [], []
        for b in range(scatter_rows // 8):
            at = pl.ds(pl.multiple_of(g * scatter_rows + b * 8, 8), 8)
            place = order_ref[at, :] - first
            hi, lo = place >> 7, place & (LANES - 1)
            live = (1 - defl_ref[at, :]).astype(F32) * coup_ref[at, :]
            values = split3(pole_ref[at, :]) + split3(live)
            for r in range(8):
                mask = hi[r : r + 1, :] == sub_hi
                left.append(
                    jnp.concatenate([jnp.where(mask, v[r : r + 1, :], 0.0) for v in values], axis=0).astype(BF16)
                )
                right.append(jnp.where(lo[r : r + 1, :] == sub_lo, 1.0, 0.0).astype(BF16))
        return acc + dot(jnp.concatenate(left, axis=1), jnp.concatenate(right, axis=1), NT)

    placed = lax.fori_loop(
        0, order_rows // scatter_rows, scatter, jnp.zeros((2 * PIECES * n_hi, LANES), F32)
    )
    part = [placed[i * n_hi : (i + 1) * n_hi, :] for i in range(2 * PIECES)]
    sq = (part[0] + part[1]) + part[2]
    num = (part[3] + part[4]) + part[5]
    num = num * jnp.where(side == 0, jnp.ones_like(sq), jnp.sqrt(sq))
    for h in range(n_hi):
        lanes = slice(h * LANES, (h + 1) * LANES)
        col_sq[:, lanes] = jnp.broadcast_to(sq[h : h + 1, :], (8, LANES))
        col_num[:, lanes] = jnp.broadcast_to(num[h : h + 1, :], (8, LANES))

    pl.semaphore_wait(meet_sem.at[0], len(near))
    for peer in middle:
        pl.semaphore_signal(meet_sem.at[1], inc=1, device_id=peer, device_id_type=MESH)

    pole = pole_ref[...]
    ahead = pltpu.roll(pole, LANES - 1, 1)
    wrapped = pltpu.roll(ahead, order_rows - 1, 0)
    lane_all = lax.broadcasted_iota(jnp.int32, (order_rows, LANES), 1)
    after = jnp.where(lane_all == LANES - 1, wrapped, ahead)
    order = order_ref[...]
    entries = split3(pole) + split3(after) + (
        (order >> 7).astype(F32), (order & (LANES - 1)).astype(F32), defl_ref[...].astype(F32),
    )
    for i, entry in enumerate(entries):
        table[:, i * LANES : (i + 1) * LANES] = entry.astype(BF16)
    lane_row = lax.broadcasted_iota(jnp.int32, (LANES, LANES), 1)
    lane_table = lax.broadcasted_iota(jnp.int32, (LANES, order_rows), 1)
    dead_mark = 65536.0

    for jb in range(triplets // LANES):
        anchor = as_column(anchor_ref[jb : jb + 1, :]).astype(jnp.int32)
        frac = as_column(frac_ref[jb : jb + 1, :])
        pick_hi = jnp.where((anchor >> 7)[:, :1] == lane_table, 1.0, 0.0).astype(BF16)
        found = dot(pick_hi, table[...], NN)
        f = [found[:, i * LANES : (i + 1) * LANES] for i in range(9)]
        pick_lo = (anchor & (LANES - 1)) == lane_row

        def chosen(value):
            return jnp.sum(jnp.where(pick_lo, value, 0.0), axis=1, keepdims=True)

        a_sq = chosen((f[0] + f[1]) + f[2])
        a_next = chosen((f[3] + f[4]) + f[5])
        target = chosen((f[6] * float(LANES) + f[7]) + f[8] * dead_mark)
        gap = a_next - a_sq
        code = jnp.where(target >= dead_mark, target - dead_mark - first.astype(F32), -dead_mark)
        at = slice(jb * LANES, (jb + 1) * LANES)
        asq_s[at, :] = jnp.broadcast_to(a_sq, (LANES, LANES))
        shift_s[at, :] = frac * gap
        code_s[at, :] = jnp.broadcast_to(code, (LANES, LANES))

    pl.semaphore_wait(meet_sem.at[1], len(middle))

    lane_wide = lax.broadcasted_iota(jnp.int32, (8, width), 1).astype(F32)

    def make_mixing(grp, g):
        chip = 1 - x if grp == 0 else x
        base = jnp.where(g < own // 16, (chip * 2 + 1 - core) * own, (chip * 2 + core) * own - own)
        parts = []
        for half in range(2):
            at = pl.ds(pl.multiple_of(base + g * 16 + half * 8, 8), 8)
            a_sq = jnp.tile(asq_s[at, :], (1, n_hi))
            shift = jnp.tile(shift_s[at, :], (1, n_hi))
            code = jnp.tile(code_s[at, :], (1, n_hi))
            den = (col_sq[...] - a_sq) - shift
            value = col_num[...] / den
            onehot = jnp.where(lane_wide == code, 1.0, 0.0)
            parts.append(jnp.where(code > -dead_mark, onehot, value))
        mix[grp, pl.ds(pl.multiple_of(g * 16, 16), 16), :] = jnp.concatenate(parts, axis=0).astype(BF16)

    def first_mixing(g, carry):
        make_mixing(0, g)
        return carry

    lax.fori_loop(0, own // 8, first_mixing, 0)
    load_old.wait()

    def product(grp, rb):
        return dot(mix[grp], old_v[pl.ds(pl.multiple_of(rb * R_TILE, R_TILE), R_TILE), :], NT)

    def on_copy(grp, rb):
        return remote(
            on_send.at[grp, rb], on_recv.at[grp, rb], on_ssem.at[grp, rb], on_rsem.at[grp, rb], sib
        )

    def cr_copy(rb):
        return remote(cr_send.at[rb], cr_recv.at[rb], cr_ssem.at[rb], cr_rsem.at[rb], across)

    def pass_across(rb):
        on_copy(0, rb).wait()
        cr_send[rb] = (hold[rb] + on_recv[0, rb].astype(F32)).astype(BF16)
        cr_copy(rb).start()

    per_rb = own // 8 // n_rb

    def other_chip(rb, carry):
        @pl.when(rb == n_rb - 1)
        def _():
            v_across.wait()
            v_fwd.start()

        value = product(0, rb)
        for q in range(per_rb):
            make_mixing(1, rb * per_rb + q)
        on_send[0, rb] = value[:own].astype(BF16)
        on_copy(0, rb).start()
        hold[rb] = value[own:]

        @pl.when(rb > 0)
        def _():
            pass_across(rb - 1)

        return carry

    lax.fori_loop(0, n_rb, other_chip, 0)
    pass_across(n_rb - 1)

    def own_chip(rb, carry):
        value = product(1, rb)
        on_send[1, rb] = value[:own].astype(BF16)
        on_copy(1, rb).start()
        merged[rb] = value[own:]
        return carry

    lax.fori_loop(0, n_rb // 2, own_chip, 0)

    def reduction(i, buf, from_y, z_in, from_z, everything):
        y_out = [
            remote(buf.at[pl.ds(y_peer(d) * n_z, n_z)], from_y.at[d - 1], ys_sem.at[i, d - 1], yr_sem.at[i, d - 1], y_dev(d))
            for d in range(1, n_y)
        ]
        z_out = [
            remote(z_in.at[z_peer(d)], from_z.at[d - 1], zs_sem.at[i, d - 1], zr_sem.at[i, d - 1], z_dev(d))
            for d in range(1, n_z)
        ]
        mine = everything.at[row]
        z_back = [remote(mine, mine, gz_ssem.at[i, d - 1], gz_rsem.at[i, d - 1], z_dev(d)) for d in range(1, n_z)]
        line = everything.at[pl.ds(y * n_z, n_z)]
        y_back = [remote(line, line, gy_ssem.at[i, d - 1], gy_rsem.at[i, d - 1], y_dev(d)) for d in range(1, n_y)]

        def start(copies):
            for copy in copies:
                copy.start()

        def wait(copies):
            for copy in copies:
                copy.wait()

        def y_to_z():
            wait(y_out)
            summed = buf[pl.ds(y * n_z, n_z)].astype(F32)
            for d in range(1, n_y):
                summed = summed + from_y[d - 1].astype(F32)
            z_in[...] = summed.astype(BF16)
            start(z_out)

        def finish():
            wait(z_out)
            summed = z_in[z].astype(F32)
            for d in range(1, n_z):
                summed = summed + from_z[d - 1].astype(F32)
            return summed

        def send_back(value):
            everything[row] = value
            start(z_back)

        def z_to_y_back():
            wait(z_back)
            start(y_back)

        return (lambda: start(y_out)), y_to_z, finish, send_back, z_to_y_back, (lambda: wait(y_back))

    red_proj = [
        reduction(i, p_buf.at[i], p_y.at[i], p_z.at[i], p_zr.at[i], p_all.at[i]) for i in range(2)
    ]
    red_gram = reduction(2, g_buf, g_y, g_z, g_zr, g_all)

    load_refl.wait()
    v_sib.wait()
    v_fwd.wait()
    for p in range(n_panels):
        for c in range(n_col):
            v_full[p, :, c * blk : (c + 1) * blk] = v_parts[c, p]
    half_at = pl.ds(pl.multiple_of(core * half_panel, half_panel), half_panel)
    gram = dot(v_full[1, :, half_at], v_full[0], TN)
    g_buf[...] = gram.reshape(n_chunks, g_chunk, panel).astype(BF16)
    red_gram[0]()

    lax.fori_loop(n_rb // 2, n_rb, own_chip, 0)

    for rb in range(n_rb):
        at = slice(rb * R_TILE, (rb + 1) * R_TILE)
        if rb == n_rb - 1:
            red_gram[1]()
        on_copy(1, rb).wait()
        cr_copy(rb).wait()
        value = merged[rb] + on_recv[1, rb].astype(F32) + cr_recv[rb].astype(F32)
        merged[rb] = value
        value_low = value.astype(BF16)
        if rb < n_rb - 1:
            for p in range(2):
                term = dot(value_low, v_full[p, at, :], NN)
                proj_acc[p] = term if rb == 0 else proj_acc[p] + term
    for i in range(2):
        p = 1 - i
        term = proj_acc[p] + dot(value_low, v_full[p, at, :], NN)
        p_buf[i] = term.reshape(n_chunks, chunk, panel).astype(BF16)
        red_proj[i][0]()

    load_tri.wait()
    upper = lax.broadcasted_iota(jnp.int32, (panel, panel), 0) <= lax.broadcasted_iota(jnp.int32, (panel, panel), 1)
    for p in range(n_panels):
        u = jnp.where(upper, tri_v[p], 0.0)
        u_high = u.astype(BF16)
        u_hi[p] = u_high
        u_lo[p] = (u - u_high.astype(F32)).astype(BF16)

    my_rows = order_rows // n_chunks
    own_at = pl.ds(pl.multiple_of(col * own, LANES), own)
    own_sq, own_shift = asq_s[own_at, :], shift_s[own_at, :]
    squares = jnp.zeros((own, LANES), F32)
    for r in range(my_rows):
        at = pl.ds(row * my_rows + r, 1)
        sq_row = pole_ref[at, :]
        weight = jnp.where(side == 0, jnp.ones_like(sq_row), jnp.sqrt(sq_row))
        num_row = (1 - defl_ref[at, :]).astype(F32) * coup_ref[at, :] * weight
        secular = num_row / ((sq_row - own_sq) - own_shift)
        squares = squares + secular * secular
    sq_own[...] = jnp.zeros((8, LANES), F32)
    for h in range(own // LANES):
        column = jnp.sum(squares[h * LANES : (h + 1) * LANES, :], axis=1, keepdims=True)
        sq_own[h : h + 1, :] = jnp.broadcast_to(column, (LANES, LANES)).T[:1, :]
    sy_copies = [
        remote(sq_own, sq_y.at[d - 1], sy_ssem.at[d - 1], sy_rsem.at[d - 1], y_dev(d)) for d in range(1, n_y)
    ]
    sz_copies = [
        remote(sq_sum, sq_z.at[d - 1], sz_ssem.at[d - 1], sz_rsem.at[d - 1], z_dev(d)) for d in range(1, n_z)
    ]
    for copy in sy_copies:
        copy.start()

    red_gram[3](red_gram[2]().astype(BF16))
    red_proj[0][1]()
    red_proj[1][1]()
    for copy in sy_copies:
        copy.wait()
    total = sq_own[...]
    for d in range(1, n_y):
        total = total + sq_y[d - 1]
    sq_sum[...] = total
    for copy in sz_copies:
        copy.start()
    red_gram[4]()

    def apply_triangle(value, p):
        high = value.astype(BF16).astype(F32)
        stacked = jnp.concatenate([high, value - high], axis=0).astype(BF16)
        by_hi = dot(stacked, u_hi[p], NT)
        by_lo = dot(stacked, u_lo[p], NT)
        return (by_hi[:chunk] + (by_hi[chunk:] + by_lo[:chunk])).astype(BF16)

    red_gram[5]()
    gram_copy = remote(g_all, gram_all.at[core], gram_ssem, gram_rsem, sib)
    gram_copy.start()
    gram_all[core] = g_all[...]
    coef_1 = apply_triangle(red_proj[0][2](), 1)
    red_proj[0][3](coef_1)
    gram_copy.wait()
    gram_rows = gram_all[...].astype(F32).reshape(panel, panel).astype(BF16)
    carried = dot(coef_1, gram_rows, NN)
    coef_0 = apply_triangle(red_proj[1][2]() - carried, 0)
    red_proj[1][3](coef_0)
    red_proj[0][4]()

    for copy in sz_copies:
        copy.wait()
    total = sq_sum[...]
    for d in range(1, n_z):
        total = total + sq_z[d - 1]
    for h in range(own // LANES):
        scale = 1.0 / jnp.sqrt(as_column(total[h : h + 1, :]) + 1e-6)
        at = pl.ds(pl.multiple_of(col * own + h * LANES, LANES), LANES)
        scale_s[h * LANES : (h + 1) * LANES, :] = jnp.where(code_s[at, :] > -dead_mark, 1.0, scale)

    red_proj[1][4]()

    for i in range(2):
        p = 1 - i
        red_proj[i][5]()
        coef_all = p_all[i].astype(F32).reshape(own, panel).astype(BF16)
        for rb in range(n_rb):
            at = slice(rb * R_TILE, (rb + 1) * R_TILE)
            value = merged[rb] - dot(coef_all, v_full[p, at, :], NT)
            if i == 1:
                out_ref[0, :, at] = (value * jnp.tile(scale_s[...], (1, R_TILE // LANES))).astype(BF16)
            else:
                merged[rb] = value


def per_device(cfg, old_vectors, reflectors, triangles, pole_sq, coupling, deflated, pole_order, anchors, root_fraction):
    n_y, n_z, n_col, triplets, width, rows, n_panels, order_rows, panel = cfg
    own = triplets // n_col
    n_rb = rows // R_TILE
    chunk = own // (n_y * n_z)
    lane_rows = lambda a: a.reshape(-1, LANES)
    dma, vmem = pltpu.SemaphoreType.DMA, pltpu.VMEM
    n_row, half = n_y * n_z, panel // 2
    scratch = [
        vmem((rows, width), BF16),
        vmem((n_panels, panel, panel), F32),
        vmem((n_col, n_panels, rows, panel // n_col), BF16),
        vmem((n_panels, rows, panel), BF16),
        vmem((n_panels, panel, panel), BF16),
        vmem((n_panels, panel, panel), BF16),
        vmem((order_rows, 9 * LANES), BF16),
        vmem((8, width), F32),
        vmem((8, width), F32),
        vmem((triplets, LANES), F32),
        vmem((triplets, LANES), F32),
        vmem((triplets, LANES), F32),
        vmem((own, LANES), F32),
        vmem((2, 2 * own, width), BF16),
        vmem((n_rb, own, R_TILE), F32),
        vmem((n_rb, own, R_TILE), F32),
        vmem((2, own, panel), F32),
        vmem((2, n_rb, own, R_TILE), BF16),
        vmem((2, n_rb, own, R_TILE), BF16),
        vmem((n_rb, own, R_TILE), BF16),
        vmem((n_rb, own, R_TILE), BF16),
        vmem((2, n_row, half // n_row, panel), BF16),
        vmem((8, LANES), F32), vmem((n_y - 1, 8, LANES), F32),
        vmem((8, LANES), F32), vmem((n_z - 1, 8, LANES), F32),
        vmem((2, n_row, chunk, panel), BF16),
        vmem((2, n_y - 1, n_z, chunk, panel), BF16),
        vmem((2, n_z, chunk, panel), BF16),
        vmem((2, n_z - 1, chunk, panel), BF16),
        vmem((2, n_row, chunk, panel), BF16),
        vmem((n_row, half // n_row, panel), BF16),
        vmem((n_y - 1, n_z, half // n_row, panel), BF16),
        vmem((n_z, half // n_row, panel), BF16),
        vmem((n_z - 1, half // n_row, panel), BF16),
        vmem((n_row, half // n_row, panel), BF16),
        dma((3,)), dma((3,)), dma((3,)),
        dma((2, n_rb)), dma((2, n_rb)), dma((n_rb,)), dma((n_rb,)), dma, dma,
        dma((n_y - 1,)), dma((n_y - 1,)), dma((n_z - 1,)), dma((n_z - 1,)),
        dma((3, n_y - 1)), dma((3, n_y - 1)),
        dma((3, n_z - 1)), dma((3, n_z - 1)),
        dma((3, n_z - 1)), dma((3, n_z - 1)),
        dma((3, n_y - 1)), dma((3, n_y - 1)), pltpu.SemaphoreType.REGULAR((2,)),
    ]
    any_spec, vmem_spec = pl.BlockSpec(memory_space=pl.ANY), pl.BlockSpec(memory_space=pltpu.VMEM)
    return pl.pallas_call(
        functools.partial(kernel, cfg),
        out_shape=jax.ShapeDtypeStruct((1, own, rows), BF16),
        in_specs=[any_spec] * 3 + [vmem_spec] * 6,
        out_specs=vmem_spec,
        scratch_shapes=scratch,
        compiler_params=pltpu.CompilerParams(
            collective_id=0, has_side_effects=True, vmem_limit_bytes=56 << 20
        ),
    )(
        old_vectors, reflectors, triangles,
        lane_rows(pole_sq), lane_rows(coupling), lane_rows(deflated), lane_rows(pole_order),
        lane_rows(anchors), lane_rows(root_fraction),
    )


def solution(mesh):
    n_row, n_col = mesh.shape["row"], mesh.shape["col"]
    n_y = 4
    n_z = n_row // n_y

    def whole(old_vectors, reflectors, triangles, pole_sq, coupling, deflated, pole_order, anchors, root_fraction):
        size, panel = reflectors.shape[2:]
        cfg = (
            n_y, n_z, n_col, anchors.shape[0], old_vectors.shape[2] // n_col, size // n_row,
            reflectors.shape[1], size // LANES, panel,
        )
        in_specs = (P("side", "row", "col"), P("side", None, "row", "col"), P("side", None, None, None)) + (P(),) * 6
        return jax.shard_map(
            functools.partial(per_device, cfg), mesh=mesh, in_specs=in_specs,
            out_specs=P("side", "col", "row"), check_vma=False,
        )(old_vectors, reflectors, triangles, pole_sq, coupling, deflated, pole_order, anchors, root_fraction)

    return whole
```

```python
import functools

import jax
import jax.numpy as jnp
from jax import lax
from jax.experimental import pallas as pl
from jax.experimental.pallas import tpu as pltpu
from jax.sharding import PartitionSpec as P

LANES = 128
R_TILE = 256
PIECES = 3
F32 = jnp.float32
BF16 = jnp.bfloat16
MESH = pl.DeviceIdType.MESH
NT = (((1,), (1,)), ((), ()))
NN = (((1,), (0,)), ((), ()))
TN = (((0,), (0,)), ((), ()))


def dot(lhs, rhs, dims):
    return lax.dot_general(lhs, rhs, dims, preferred_element_type=F32)


def split3(value):
    high = value.astype(BF16).astype(F32)
    rest = value - high
    middle = rest.astype(BF16).astype(F32)
    return high, middle, rest - middle


def as_column(row):
    return jnp.broadcast_to(row.astype(F32), (LANES, LANES)).T


def kernel(
    cfg,
    old_hbm, refl_hbm, tri_hbm, pole_ref, coup_ref, defl_ref, order_ref, anchor_ref, frac_ref,
    out_ref,
    old_v, tri_v, v_parts, v_full, u_hi, u_lo, table, col_sq, col_num, asq_s, shift_s, code_s, scale_s,
    mix, hold, merged, proj_acc, on_send, on_recv, cr_send, cr_recv, gram_all,
    sq_own, sq_y, sq_sum, sq_z,
    p_buf, p_y, p_z, p_zr, p_all, g_buf, g_y, g_z, g_zr, g_all,
    load_sem, v_send, v_recv, on_ssem, on_rsem, cr_ssem, cr_rsem, gram_ssem, gram_rsem,
    sy_ssem, sy_rsem, sz_ssem, sz_rsem,
    ys_sem, yr_sem, zs_sem, zr_sem, b_ssem, b_rsem, meet_sem,
):
    n_y, n_z, n_col, triplets, width, rows, n_panels, order_rows, panel = cfg
    own = triplets // n_col
    half_rows = n_y * n_z // 2
    n_chunks = n_y * n_z
    n_hi = width // LANES
    n_rb = rows // R_TILE
    chunk = own // n_chunks
    blk = panel // n_col
    half_panel = panel // 2
    g_chunk = 2 * blk // n_chunks
    scatter_rows = order_rows // 2

    side = lax.axis_index("side")
    row = lax.axis_index("row")
    col = lax.axis_index("col")
    y, z = row // n_z, row % n_z
    x, core = col // 2, col % 2
    sib = {"col": x * 2 + 1 - core}
    across = {"col": (1 - x) * 2 + core}

    def y_peer(d):
        return lax.rem(y + d, n_y)

    def z_peer(d):
        return lax.rem(z + d, n_z)

    def y_dev(d):
        return {"row": y_peer(d) * n_z + z}

    def z_dev(d):
        return {"row": y * n_z + z_peer(d)}

    y_near = sorted({1, n_y - 1})
    z_near = sorted({1, n_z - 1})
    z_mid = sorted({d % n_z for d in (1, -1, 2, -2)} - {0})
    near = [y_dev(d) for d in y_near] + [z_dev(d) for d in z_near]
    middle = [z_dev(d) for d in z_mid]
    peers = [sib, across] + near
    barrier = pltpu.get_barrier_semaphore()
    for peer in peers:
        pl.semaphore_signal(barrier, inc=1, device_id=peer, device_id_type=MESH)

    load_refl = pltpu.make_async_copy(refl_hbm.at[0], v_parts.at[col], load_sem.at[1])
    load_old = pltpu.make_async_copy(old_hbm.at[0], old_v, load_sem.at[0])
    load_tri = pltpu.make_async_copy(tri_hbm.at[0], tri_v, load_sem.at[2])
    load_refl.start()
    load_old.start()

    def remote(src, dst, ssem, rsem, peer):
        return pltpu.make_async_remote_copy(
            src_ref=src, dst_ref=dst, send_sem=ssem, recv_sem=rsem, device_id=peer, device_id_type=MESH
        )

    first = row // half_rows * (width * n_col) + col * width
    sub_hi = lax.broadcasted_iota(jnp.int32, (n_hi, LANES), 0)
    sub_lo = lax.broadcasted_iota(jnp.int32, (LANES, LANES), 0)

    def scatter(g, acc):
        left, right = [], []
        for b in range(scatter_rows // 8):
            at = pl.ds(pl.multiple_of(g * scatter_rows + b * 8, 8), 8)
            place = order_ref[at, :] - first
            hi, lo = place >> 7, place & (LANES - 1)
            live = (1 - defl_ref[at, :]).astype(F32) * coup_ref[at, :]
            values = split3(pole_ref[at, :]) + split3(live)
            for r in range(8):
                mask = hi[r : r + 1, :] == sub_hi
                left.append(
                    jnp.concatenate([jnp.where(mask, v[r : r + 1, :], 0.0) for v in values], axis=0).astype(BF16)
                )
                right.append(jnp.where(lo[r : r + 1, :] == sub_lo, 1.0, 0.0).astype(BF16))
        return acc + dot(jnp.concatenate(left, axis=1), jnp.concatenate(right, axis=1), NT)

    placed = scatter(0, jnp.zeros((2 * PIECES * n_hi, LANES), F32))

    pl.semaphore_wait(barrier, len(peers))
    for peer in near:
        pl.semaphore_signal(meet_sem.at[0], inc=1, device_id=peer, device_id_type=MESH)

    v_fwd_at = (1 - x) * 2 + core
    v_across, v_fwd = [], []
    for p in range(2):
        v_across.append(remote(refl_hbm.at[0, p], v_parts.at[col, p], v_send.at[p], v_recv.at[p], across))
        v_fwd.append(
            remote(v_parts.at[v_fwd_at, p], v_parts.at[v_fwd_at, p], v_send.at[2 + p], v_recv.at[2 + p], sib)
        )
    v_sib = remote(refl_hbm.at[0], v_parts.at[col], v_send.at[4], v_recv.at[4], sib)
    v_across[0].start()
    v_sib.start()
    load_tri.start()

    placed = scatter(1, placed)
    part = [placed[i * n_hi : (i + 1) * n_hi, :] for i in range(2 * PIECES)]
    sq = (part[0] + part[1]) + part[2]
    num = (part[3] + part[4]) + part[5]
    num = num * jnp.where(side == 0, jnp.ones_like(sq), jnp.sqrt(sq))
    for h in range(n_hi):
        lanes = slice(h * LANES, (h + 1) * LANES)
        col_sq[:, lanes] = jnp.broadcast_to(sq[h : h + 1, :], (8, LANES))
        col_num[:, lanes] = jnp.broadcast_to(num[h : h + 1, :], (8, LANES))

    pole = pole_ref[...]
    ahead = pltpu.roll(pole, LANES - 1, 1)
    wrapped = pltpu.roll(ahead, order_rows - 1, 0)
    lane_all = lax.broadcasted_iota(jnp.int32, (order_rows, LANES), 1)
    after = jnp.where(lane_all == LANES - 1, wrapped, ahead)
    order = order_ref[...]
    entries = split3(pole) + split3(after) + (
        (order >> 7).astype(F32), (order & (LANES - 1)).astype(F32), defl_ref[...].astype(F32),
    )
    for i, entry in enumerate(entries):
        table[:, i * LANES : (i + 1) * LANES] = entry.astype(BF16)
    lane_row = lax.broadcasted_iota(jnp.int32, (LANES, LANES), 1)
    lane_table = lax.broadcasted_iota(jnp.int32, (LANES, order_rows), 1)
    dead_mark = 65536.0

    for jb in range(triplets // LANES):
        anchor = as_column(anchor_ref[jb : jb + 1, :]).astype(jnp.int32)
        frac = as_column(frac_ref[jb : jb + 1, :])
        pick_hi = jnp.where((anchor >> 7)[:, :1] == lane_table, 1.0, 0.0).astype(BF16)
        found = dot(pick_hi, table[...], NN)
        f = [found[:, i * LANES : (i + 1) * LANES] for i in range(9)]
        pick_lo = (anchor & (LANES - 1)) == lane_row

        def chosen(value):
            return jnp.sum(jnp.where(pick_lo, value, 0.0), axis=1, keepdims=True)

        a_sq = chosen((f[0] + f[1]) + f[2])
        a_next = chosen((f[3] + f[4]) + f[5])
        target = chosen((f[6] * float(LANES) + f[7]) + f[8] * dead_mark)
        gap = a_next - a_sq
        code = jnp.where(target >= dead_mark, target - dead_mark - first.astype(F32), -dead_mark)
        at = slice(jb * LANES, (jb + 1) * LANES)
        asq_s[at, :] = jnp.broadcast_to(a_sq, (LANES, LANES))
        shift_s[at, :] = frac * gap
        code_s[at, :] = jnp.broadcast_to(code, (LANES, LANES))

    v_across[1].start()
    pl.semaphore_wait(meet_sem.at[0], len(near))
    for peer in middle:
        pl.semaphore_signal(meet_sem.at[1], inc=1, device_id=peer, device_id_type=MESH)

    lane_wide = lax.broadcasted_iota(jnp.int32, (8, width), 1).astype(F32)

    def make_mixing(grp, g):
        chip = 1 - x if grp == 0 else x
        base = jnp.where(g < own // 16, (chip * 2 + 1 - core) * own, (chip * 2 + core) * own - own)
        parts = []
        for half in range(2):
            at = pl.ds(pl.multiple_of(base + g * 16 + half * 8, 8), 8)
            a_sq = jnp.tile(asq_s[at, :], (1, n_hi))
            shift = jnp.tile(shift_s[at, :], (1, n_hi))
            code = jnp.tile(code_s[at, :], (1, n_hi))
            den = (col_sq[...] - a_sq) - shift
            value = col_num[...] / den
            onehot = jnp.where(lane_wide == code, 1.0, 0.0)
            parts.append(jnp.where(code > -dead_mark, onehot, value))
        mix[grp, pl.ds(pl.multiple_of(g * 16, 16), 16), :] = jnp.concatenate(parts, axis=0).astype(BF16)

    def first_mixing(g, carry):
        make_mixing(0, g)
        return carry

    lax.fori_loop(0, own // 8, first_mixing, 0)
    load_old.wait()

    def product(grp, rb):
        return dot(mix[grp], old_v[pl.ds(pl.multiple_of(rb * R_TILE, R_TILE), R_TILE), :], NT)

    def on_copy(grp, rb):
        return remote(
            on_send.at[grp, rb], on_recv.at[grp, rb], on_ssem.at[grp, rb], on_rsem.at[grp, rb], sib
        )

    def cr_copy(rb):
        return remote(cr_send.at[rb], cr_recv.at[rb], cr_ssem.at[rb], cr_rsem.at[rb], across)

    def pass_across(rb):
        on_copy(0, rb).wait()
        cr_send[rb] = (hold[rb] + on_recv[0, rb].astype(F32)).astype(BF16)
        cr_copy(rb).start()

    far = [(dy, dz) for dy in range(n_y) for dz in range(n_z) if dy or dz]
    far.sort(key=lambda d: -(min(d[0], n_y - d[0]) + min(d[1], n_z - d[1])))

    def far_dev(dy, dz):
        return {"row": y_peer(dy) * n_z + z_peer(dz)}

    def reduction(i, buf, from_y, z_in, from_z, everything):
        y_out = [
            remote(buf.at[pl.ds(y_peer(d) * n_z, n_z)], from_y.at[d - 1], ys_sem.at[i, d - 1], yr_sem.at[i, d - 1], y_dev(d))
            for d in range(1, n_y)
        ]
        z_out = [
            remote(z_in.at[z_peer(d)], from_z.at[d - 1], zs_sem.at[i, d - 1], zr_sem.at[i, d - 1], z_dev(d))
            for d in range(1, n_z)
        ]
        mine = everything.at[row]
        back = [remote(mine, mine, b_ssem.at[i, k], b_rsem.at[i, k], far_dev(dy, dz)) for k, (dy, dz) in enumerate(far)]

        def start(copies):
            for copy in copies:
                copy.start()

        def wait(copies):
            for copy in copies:
                copy.wait()

        def y_to_z():
            wait(y_out)
            summed = buf[pl.ds(y * n_z, n_z)].astype(F32)
            for d in range(1, n_y):
                summed = summed + from_y[d - 1].astype(F32)
            z_in[...] = summed.astype(BF16)
            start(z_out)

        def finish():
            wait(z_out)
            summed = z_in[z].astype(F32)
            for d in range(1, n_z):
                summed = summed + from_z[d - 1].astype(F32)
            return summed

        def send_back(value):
            everything[row] = value
            start(back)

        return (lambda: start(y_out)), y_to_z, finish, send_back, (lambda: wait(back))

    red_proj = [
        reduction(i, p_buf.at[i], p_y.at[i], p_z.at[i], p_zr.at[i], p_all.at[i]) for i in range(2)
    ]
    red_gram = reduction(2, g_buf, g_y, g_z, g_zr, g_all)

    per_rb = own // 8 // n_rb

    def assemble(p):
        for c in range(n_col):
            v_full[p, :, c * blk : (c + 1) * blk] = v_parts[c, p]

    v_across[0].wait()
    v_fwd[0].start()

    def other_chip(rb, carry):
        @pl.when(rb == n_rb - 1)
        def _():
            v_across[1].wait()
            v_fwd[1].start()

        @pl.when(rb == 1)
        def _():
            load_refl.wait()
            v_sib.wait()
            v_fwd[0].wait()
            assemble(0)
            gram = dot(v_parts[col, 1], v_full[0], TN)
            gram = jnp.concatenate([gram[:, :half_panel], gram[:, half_panel:]], axis=0)
            g_buf[...] = gram.reshape(n_chunks, g_chunk, half_panel).astype(BF16)
            red_gram[0]()

        value = product(0, rb)
        for q in range(per_rb):
            make_mixing(1, rb * per_rb + q)
        on_send[0, rb] = value[:own].astype(BF16)
        on_copy(0, rb).start()
        hold[rb] = value[own:]

        @pl.when(rb > 0)
        def _():
            pass_across(rb - 1)

        return carry

    lax.fori_loop(0, n_rb, other_chip, 0)
    pass_across(n_rb - 1)

    my_rows = order_rows // n_chunks
    own_at = pl.ds(pl.multiple_of(col * own, LANES), own)
    own_sq, own_shift = asq_s[own_at, :], shift_s[own_at, :]
    squares = jnp.zeros((own, LANES), F32)
    for r in range(my_rows):
        at = pl.ds(row * my_rows + r, 1)
        sq_row = pole_ref[at, :]
        weight = jnp.where(side == 0, jnp.ones_like(sq_row), jnp.sqrt(sq_row))
        num_row = (1 - defl_ref[at, :]).astype(F32) * coup_ref[at, :] * weight
        secular = num_row / ((sq_row - own_sq) - own_shift)
        squares = squares + secular * secular
    sq_own[...] = jnp.zeros((8, LANES), F32)
    for h in range(own // LANES):
        column = jnp.sum(squares[h * LANES : (h + 1) * LANES, :], axis=1, keepdims=True)
        sq_own[h : h + 1, :] = jnp.broadcast_to(column, (LANES, LANES)).T[:1, :]
    sy_copies = [
        remote(sq_own, sq_y.at[d - 1], sy_ssem.at[d - 1], sy_rsem.at[d - 1], y_dev(d)) for d in range(1, n_y)
    ]
    sz_copies = [
        remote(sq_sum, sq_z.at[d - 1], sz_ssem.at[d - 1], sz_rsem.at[d - 1], z_dev(d)) for d in range(1, n_z)
    ]
    pl.semaphore_wait(meet_sem.at[1], len(middle))
    for copy in sy_copies:
        copy.start()
    red_gram[1]()

    def own_chip(rb, carry):
        value = product(1, rb)
        on_send[1, rb] = value[:own].astype(BF16)
        on_copy(1, rb).start()
        merged[rb] = value[own:]
        return carry

    lax.fori_loop(0, n_rb, own_chip, 0)
    v_fwd[1].wait()
    assemble(1)
    red_gram[3](red_gram[2]().astype(BF16))

    for rb in range(n_rb):
        at = slice(rb * R_TILE, (rb + 1) * R_TILE)
        on_copy(1, rb).wait()
        cr_copy(rb).wait()
        value = merged[rb] + on_recv[1, rb].astype(F32) + cr_recv[rb].astype(F32)
        merged[rb] = value
        value_low = value.astype(BF16)
        if rb < n_rb - 1:
            for p in range(2):
                term = dot(value_low, v_full[p, at, :], NN)
                proj_acc[p] = term if rb == 0 else proj_acc[p] + term
    for i in range(2):
        p = 1 - i
        term = proj_acc[p] + dot(value_low, v_full[p, at, :], NN)
        p_buf[i] = term.reshape(n_chunks, chunk, panel).astype(BF16)
        red_proj[i][0]()

    load_tri.wait()
    upper = lax.broadcasted_iota(jnp.int32, (panel, panel), 0) <= lax.broadcasted_iota(jnp.int32, (panel, panel), 1)
    for p in range(n_panels):
        u = jnp.where(upper, tri_v[p], 0.0)
        u_high = u.astype(BF16)
        u_hi[p] = u_high
        u_lo[p] = (u - u_high.astype(F32)).astype(BF16)

    for copy in sy_copies:
        copy.wait()
    total = sq_own[...]
    for d in range(1, n_y):
        total = total + sq_y[d - 1]
    sq_sum[...] = total
    for copy in sz_copies:
        copy.start()

    red_proj[0][1]()
    red_proj[1][1]()

    def apply_triangle(value, p):
        high = value.astype(BF16).astype(F32)
        stacked = jnp.concatenate([high, value - high], axis=0).astype(BF16)
        by_hi = dot(stacked, u_hi[p], NT)
        by_lo = dot(stacked, u_lo[p], NT)
        return (by_hi[:chunk] + (by_hi[chunk:] + by_lo[:chunk])).astype(BF16)

    red_gram[4]()
    diagonal = {"col": (1 - x) * 2 + 1 - core}
    gram_copies = [
        remote(g_all, gram_all.at[col], gram_ssem.at[i], gram_rsem.at[i], peer)
        for i, peer in enumerate((across, diagonal, sib))
    ]
    for copy in gram_copies:
        copy.start()
    gram_all[col] = g_all[...]
    coef_1 = apply_triangle(red_proj[0][2](), 1)
    red_proj[0][3](coef_1)
    gram_rows = []
    for copy in gram_copies:
        copy.wait()
    for c in range(n_col):
        quarter = gram_all[c].astype(F32).reshape(2 * blk, half_panel)
        gram_rows.append(jnp.concatenate([quarter[:blk], quarter[blk:]], axis=1))
    gram_rows = jnp.concatenate(gram_rows, axis=0).astype(BF16)
    carried = dot(coef_1, gram_rows, NN)
    coef_0 = apply_triangle(red_proj[1][2]() - carried, 0)
    red_proj[1][3](coef_0)
    for copy in sz_copies:
        copy.wait()
    total = sq_sum[...]
    for d in range(1, n_z):
        total = total + sq_z[d - 1]
    for h in range(own // LANES):
        scale = 1.0 / jnp.sqrt(as_column(total[h : h + 1, :]) + 1e-6)
        at = pl.ds(pl.multiple_of(col * own + h * LANES, LANES), LANES)
        scale_s[h * LANES : (h + 1) * LANES, :] = jnp.where(code_s[at, :] > -dead_mark, 1.0, scale)

    for i in range(2):
        p = 1 - i
        red_proj[i][4]()
        coef_all = p_all[i].astype(F32).reshape(own, panel).astype(BF16)
        for rb in range(n_rb):
            at = slice(rb * R_TILE, (rb + 1) * R_TILE)
            value = merged[rb] - dot(coef_all, v_full[p, at, :], NT)
            if i == 1:
                out_ref[0, :, at] = (value * jnp.tile(scale_s[...], (1, R_TILE // LANES))).astype(BF16)
            else:
                merged[rb] = value


def per_device(cfg, old_vectors, reflectors, triangles, pole_sq, coupling, deflated, pole_order, anchors, root_fraction):
    n_y, n_z, n_col, triplets, width, rows, n_panels, order_rows, panel = cfg
    own = triplets // n_col
    n_rb = rows // R_TILE
    chunk = own // (n_y * n_z)
    lane_rows = lambda a: a.reshape(-1, LANES)
    dma, vmem = pltpu.SemaphoreType.DMA, pltpu.VMEM
    n_row, half = n_y * n_z, panel // 2
    g_chunk = 2 * (panel // n_col) // n_row
    scratch = [
        vmem((rows, width), BF16),
        vmem((n_panels, panel, panel), F32),
        vmem((n_col, n_panels, rows, panel // n_col), BF16),
        vmem((n_panels, rows, panel), BF16),
        vmem((n_panels, panel, panel), BF16),
        vmem((n_panels, panel, panel), BF16),
        vmem((order_rows, 9 * LANES), BF16),
        vmem((8, width), F32),
        vmem((8, width), F32),
        vmem((triplets, LANES), F32),
        vmem((triplets, LANES), F32),
        vmem((triplets, LANES), F32),
        vmem((own, LANES), F32),
        vmem((2, 2 * own, width), BF16),
        vmem((n_rb, own, R_TILE), F32),
        vmem((n_rb, own, R_TILE), F32),
        vmem((2, own, panel), F32),
        vmem((2, n_rb, own, R_TILE), BF16),
        vmem((2, n_rb, own, R_TILE), BF16),
        vmem((n_rb, own, R_TILE), BF16),
        vmem((n_rb, own, R_TILE), BF16),
        vmem((n_col, n_row, g_chunk, half), BF16),
        vmem((8, LANES), F32), vmem((n_y - 1, 8, LANES), F32),
        vmem((8, LANES), F32), vmem((n_z - 1, 8, LANES), F32),
        vmem((2, n_row, chunk, panel), BF16),
        vmem((2, n_y - 1, n_z, chunk, panel), BF16),
        vmem((2, n_z, chunk, panel), BF16),
        vmem((2, n_z - 1, chunk, panel), BF16),
        vmem((2, n_row, chunk, panel), BF16),
        vmem((n_row, g_chunk, half), BF16),
        vmem((n_y - 1, n_z, g_chunk, half), BF16),
        vmem((n_z, g_chunk, half), BF16),
        vmem((n_z - 1, g_chunk, half), BF16),
        vmem((n_row, g_chunk, half), BF16),
        dma((3,)), dma((5,)), dma((5,)),
        dma((2, n_rb)), dma((2, n_rb)), dma((n_rb,)), dma((n_rb,)), dma((3,)), dma((3,)),
        dma((n_y - 1,)), dma((n_y - 1,)), dma((n_z - 1,)), dma((n_z - 1,)),
        dma((3, n_y - 1)), dma((3, n_y - 1)),
        dma((3, n_z - 1)), dma((3, n_z - 1)),
        dma((3, n_row - 1)), dma((3, n_row - 1)), pltpu.SemaphoreType.REGULAR((2,)),
    ]
    any_spec, vmem_spec = pl.BlockSpec(memory_space=pl.ANY), pl.BlockSpec(memory_space=pltpu.VMEM)
    return pl.pallas_call(
        functools.partial(kernel, cfg),
        out_shape=jax.ShapeDtypeStruct((1, own, rows), BF16),
        in_specs=[any_spec] * 3 + [vmem_spec] * 6,
        out_specs=vmem_spec,
        scratch_shapes=scratch,
        compiler_params=pltpu.CompilerParams(
            collective_id=0, has_side_effects=True, vmem_limit_bytes=56 << 20
        ),
    )(
        old_vectors, reflectors, triangles,
        lane_rows(pole_sq), lane_rows(coupling), lane_rows(deflated), lane_rows(pole_order),
        lane_rows(anchors), lane_rows(root_fraction),
    )


def solution(mesh):
    n_row, n_col = mesh.shape["row"], mesh.shape["col"]
    n_y = 4
    n_z = n_row // n_y

    def whole(old_vectors, reflectors, triangles, pole_sq, coupling, deflated, pole_order, anchors, root_fraction):
        size, panel = reflectors.shape[2:]
        cfg = (
            n_y, n_z, n_col, anchors.shape[0], old_vectors.shape[2] // n_col, size // n_row,
            reflectors.shape[1], size // LANES, panel,
        )
        in_specs = (P("side", "row", "col"), P("side", None, "row", "col"), P("side", None, None, None)) + (P(),) * 6
        return jax.shard_map(
            functools.partial(per_device, cfg), mesh=mesh, in_specs=in_specs,
            out_specs=P("side", "col", "row"), check_vma=False,
        )(old_vectors, reflectors, triangles, pole_sq, coupling, deflated, pole_order, anchors, root_fraction)

    return whole
```

```python
import functools

import jax
import jax.numpy as jnp
from jax import lax
from jax.experimental import pallas as pl
from jax.experimental.pallas import tpu as pltpu
from jax.sharding import PartitionSpec as P

LANES = 128
R_TILE = 256
PIECES = 3
F32 = jnp.float32
BF16 = jnp.bfloat16
MESH = pl.DeviceIdType.MESH
NT = (((1,), (1,)), ((), ()))
NN = (((1,), (0,)), ((), ()))
TN = (((0,), (0,)), ((), ()))


def dot(lhs, rhs, dims):
    return lax.dot_general(lhs, rhs, dims, preferred_element_type=F32)


def split3(value):
    high = value.astype(BF16).astype(F32)
    rest = value - high
    middle = rest.astype(BF16).astype(F32)
    return high, middle, rest - middle


def as_column(row):
    return jnp.broadcast_to(row.astype(F32), (LANES, LANES)).T


def kernel(
    cfg,
    old_hbm, refl_hbm, tri_hbm, pole_ref, coup_ref, defl_ref, order_ref, anchor_ref, frac_ref,
    out_ref,
    old_v, tri_v, v_parts, v_full, u_hi, u_lo, table, col_sq, col_num, asq_s, shift_s, code_s, scale_s,
    mix, hold, merged, proj_acc, on_send, on_recv, cr_send, cr_recv, gram_all,
    sq_own, sq_y, sq_sum, sq_z,
    p_buf, p_y, p_z, p_zr, p_all, g_buf, g_y, g_z, g_zr, g_all,
    load_sem, v_send, v_recv, on_ssem, on_rsem, cr_ssem, cr_rsem, gram_ssem, gram_rsem,
    sy_ssem, sy_rsem, sz_ssem, sz_rsem,
    ys_sem, yr_sem, zs_sem, zr_sem, b_ssem, b_rsem, meet_sem,
):
    n_y, n_z, n_col, triplets, width, rows, n_panels, order_rows, panel = cfg
    own = triplets // n_col
    half_rows = n_y * n_z // 2
    n_chunks = n_y * n_z
    n_hi = width // LANES
    n_rb = rows // R_TILE
    chunk = own // n_chunks
    blk = panel // n_col
    half_panel = panel // 2
    g_chunk = 2 * blk // n_chunks
    scatter_rows = order_rows // 2

    side = lax.axis_index("side")
    row = lax.axis_index("row")
    col = lax.axis_index("col")
    y, z = row // n_z, row % n_z
    x, core = col // 2, col % 2
    sib = {"col": x * 2 + 1 - core}
    across = {"col": (1 - x) * 2 + core}

    def y_peer(d):
        return lax.rem(y + d, n_y)

    def z_peer(d):
        return lax.rem(z + d, n_z)

    def y_dev(d):
        return {"row": y_peer(d) * n_z + z}

    def z_dev(d):
        return {"row": y * n_z + z_peer(d)}

    y_near = sorted({1, n_y - 1})
    z_near = sorted({1, n_z - 1})
    z_mid = sorted({d % n_z for d in (1, -1, 2, -2)} - {0})
    near = [y_dev(d) for d in y_near] + [z_dev(d) for d in z_near]
    middle = [z_dev(d) for d in z_mid]
    peers = [sib, across] + near
    barrier = pltpu.get_barrier_semaphore()
    for peer in peers:
        pl.semaphore_signal(barrier, inc=1, device_id=peer, device_id_type=MESH)

    load_refl = pltpu.make_async_copy(refl_hbm.at[0], v_parts.at[col], load_sem.at[1])
    load_old = pltpu.make_async_copy(old_hbm.at[0], old_v, load_sem.at[0])
    load_tri = pltpu.make_async_copy(tri_hbm.at[0], tri_v, load_sem.at[2])
    load_refl.start()
    load_old.start()

    def remote(src, dst, ssem, rsem, peer):
        return pltpu.make_async_remote_copy(
            src_ref=src, dst_ref=dst, send_sem=ssem, recv_sem=rsem, device_id=peer, device_id_type=MESH
        )

    first = row // half_rows * (width * n_col) + col * width
    sub_hi = lax.broadcasted_iota(jnp.int32, (n_hi, LANES), 0)
    sub_lo = lax.broadcasted_iota(jnp.int32, (LANES, LANES), 0)

    def scatter(g, acc):
        left, right = [], []
        for b in range(scatter_rows // 8):
            at = pl.ds(pl.multiple_of(g * scatter_rows + b * 8, 8), 8)
            place = order_ref[at, :] - first
            hi, lo = place >> 7, place & (LANES - 1)
            live = (1 - defl_ref[at, :]).astype(F32) * coup_ref[at, :]
            values = split3(pole_ref[at, :]) + split3(live)
            for r in range(8):
                mask = hi[r : r + 1, :] == sub_hi
                left.append(
                    jnp.concatenate([jnp.where(mask, v[r : r + 1, :], 0.0) for v in values], axis=0).astype(BF16)
                )
                right.append(jnp.where(lo[r : r + 1, :] == sub_lo, 1.0, 0.0).astype(BF16))
        return acc + dot(jnp.concatenate(left, axis=1), jnp.concatenate(right, axis=1), NT)

    placed = scatter(0, jnp.zeros((2 * PIECES * n_hi, LANES), F32))

    pl.semaphore_wait(barrier, len(peers))
    for peer in near:
        pl.semaphore_signal(meet_sem.at[0], inc=1, device_id=peer, device_id_type=MESH)

    v_fwd_at = (1 - x) * 2 + core
    v_across, v_fwd = [], []
    for p in range(2):
        v_across.append(remote(refl_hbm.at[0, p], v_parts.at[col, p], v_send.at[p], v_recv.at[p], across))
        v_fwd.append(
            remote(v_parts.at[v_fwd_at, p], v_parts.at[v_fwd_at, p], v_send.at[2 + p], v_recv.at[2 + p], sib)
        )
    v_sib = remote(refl_hbm.at[0], v_parts.at[col], v_send.at[4], v_recv.at[4], sib)
    v_across[0].start()
    v_sib.start()
    load_tri.start()

    placed = scatter(1, placed)
    part = [placed[i * n_hi : (i + 1) * n_hi, :] for i in range(2 * PIECES)]
    sq = (part[0] + part[1]) + part[2]
    num = (part[3] + part[4]) + part[5]
    num = num * jnp.where(side == 0, jnp.ones_like(sq), jnp.sqrt(sq))
    for h in range(n_hi):
        lanes = slice(h * LANES, (h + 1) * LANES)
        col_sq[:, lanes] = jnp.broadcast_to(sq[h : h + 1, :], (8, LANES))
        col_num[:, lanes] = jnp.broadcast_to(num[h : h + 1, :], (8, LANES))

    pole = pole_ref[...]
    ahead = pltpu.roll(pole, LANES - 1, 1)
    wrapped = pltpu.roll(ahead, order_rows - 1, 0)
    lane_all = lax.broadcasted_iota(jnp.int32, (order_rows, LANES), 1)
    after = jnp.where(lane_all == LANES - 1, wrapped, ahead)
    order = order_ref[...]
    entries = split3(pole) + split3(after) + (
        (order >> 7).astype(F32), (order & (LANES - 1)).astype(F32), defl_ref[...].astype(F32),
    )
    for i, entry in enumerate(entries):
        table[:, i * LANES : (i + 1) * LANES] = entry.astype(BF16)
    lane_row = lax.broadcasted_iota(jnp.int32, (LANES, LANES), 1)
    lane_table = lax.broadcasted_iota(jnp.int32, (LANES, order_rows), 1)
    dead_mark = 65536.0

    for jb in range(triplets // LANES):
        anchor = as_column(anchor_ref[jb : jb + 1, :]).astype(jnp.int32)
        frac = as_column(frac_ref[jb : jb + 1, :])
        pick_hi = jnp.where((anchor >> 7)[:, :1] == lane_table, 1.0, 0.0).astype(BF16)
        found = dot(pick_hi, table[...], NN)
        f = [found[:, i * LANES : (i + 1) * LANES] for i in range(9)]
        pick_lo = (anchor & (LANES - 1)) == lane_row

        def chosen(value):
            return jnp.sum(jnp.where(pick_lo, value, 0.0), axis=1, keepdims=True)

        a_sq = chosen((f[0] + f[1]) + f[2])
        a_next = chosen((f[3] + f[4]) + f[5])
        target = chosen((f[6] * float(LANES) + f[7]) + f[8] * dead_mark)
        gap = a_next - a_sq
        code = jnp.where(target >= dead_mark, target - dead_mark - first.astype(F32), -dead_mark)
        at = slice(jb * LANES, (jb + 1) * LANES)
        asq_s[at, :] = jnp.broadcast_to(a_sq, (LANES, LANES))
        shift_s[at, :] = frac * gap
        code_s[at, :] = jnp.broadcast_to(code, (LANES, LANES))

    v_across[1].start()
    pl.semaphore_wait(meet_sem.at[0], len(near))
    for peer in middle:
        pl.semaphore_signal(meet_sem.at[1], inc=1, device_id=peer, device_id_type=MESH)

    lane_wide = lax.broadcasted_iota(jnp.int32, (8, width), 1).astype(F32)

    def make_mixing(grp, g):
        chip = 1 - x if grp == 0 else x
        base = jnp.where(g < own // 16, (chip * 2 + 1 - core) * own, (chip * 2 + core) * own - own)
        parts = []
        for half in range(2):
            at = pl.ds(pl.multiple_of(base + g * 16 + half * 8, 8), 8)
            a_sq = jnp.tile(asq_s[at, :], (1, n_hi))
            shift = jnp.tile(shift_s[at, :], (1, n_hi))
            code = jnp.tile(code_s[at, :], (1, n_hi))
            den = (col_sq[...] - a_sq) - shift
            value = col_num[...] / den
            onehot = jnp.where(lane_wide == code, 1.0, 0.0)
            parts.append(jnp.where(code > -dead_mark, onehot, value))
        mix[grp, pl.ds(pl.multiple_of(g * 16, 16), 16), :] = jnp.concatenate(parts, axis=0).astype(BF16)

    def first_mixing(g, carry):
        make_mixing(0, g)
        return carry

    lax.fori_loop(0, own // 8, first_mixing, 0)
    load_old.wait()

    def product(grp, rb):
        return dot(mix[grp], old_v[pl.ds(pl.multiple_of(rb * R_TILE, R_TILE), R_TILE), :], NT)

    def on_copy(grp, rb):
        return remote(
            on_send.at[grp, rb], on_recv.at[grp, rb], on_ssem.at[grp, rb], on_rsem.at[grp, rb], sib
        )

    def cr_copy(rb):
        return remote(cr_send.at[rb], cr_recv.at[rb], cr_ssem.at[rb], cr_rsem.at[rb], across)

    def pass_across(rb):
        on_copy(0, rb).wait()
        cr_send[rb] = (hold[rb] + on_recv[0, rb].astype(F32)).astype(BF16)
        cr_copy(rb).start()

    far = [(dy, dz) for dy in range(n_y) for dz in range(n_z) if dy or dz]
    far.sort(key=lambda d: -(min(d[0], n_y - d[0]) + min(d[1], n_z - d[1])))

    def far_dev(dy, dz):
        return {"row": y_peer(dy) * n_z + z_peer(dz)}

    def reduction(i, buf, from_y, z_in, from_z, everything):
        y_out = [
            remote(buf.at[pl.ds(y_peer(d) * n_z, n_z)], from_y.at[d - 1], ys_sem.at[i, d - 1], yr_sem.at[i, d - 1], y_dev(d))
            for d in range(1, n_y)
        ]
        z_out = [
            remote(z_in.at[z_peer(d)], from_z.at[d - 1], zs_sem.at[i, d - 1], zr_sem.at[i, d - 1], z_dev(d))
            for d in range(1, n_z)
        ]
        mine = everything.at[row]
        back = [remote(mine, mine, b_ssem.at[i, k], b_rsem.at[i, k], far_dev(dy, dz)) for k, (dy, dz) in enumerate(far)]

        def start(copies):
            for copy in copies:
                copy.start()

        def wait(copies):
            for copy in copies:
                copy.wait()

        def y_to_z():
            wait(y_out)
            summed = buf[pl.ds(y * n_z, n_z)].astype(F32)
            for d in range(1, n_y):
                summed = summed + from_y[d - 1].astype(F32)
            z_in[...] = summed.astype(BF16)
            start(z_out)

        def finish():
            wait(z_out)
            summed = z_in[z].astype(F32)
            for d in range(1, n_z):
                summed = summed + from_z[d - 1].astype(F32)
            return summed

        def send_back(value):
            everything[row] = value
            start(back)

        return (lambda: start(y_out)), y_to_z, finish, send_back, (lambda: wait(back))

    red_proj = [
        reduction(i, p_buf.at[i], p_y.at[i], p_z.at[i], p_zr.at[i], p_all.at[i]) for i in range(2)
    ]
    red_gram = reduction(2, g_buf, g_y, g_z, g_zr, g_all)

    per_rb = own // 8 // n_rb

    def assemble(p):
        for c in range(n_col):
            v_full[p, :, c * blk : (c + 1) * blk] = v_parts[c, p]

    v_across[0].wait()
    v_fwd[0].start()

    def other_chip(rb, carry):
        @pl.when(rb == n_rb - 1)
        def _():
            v_across[1].wait()
            v_fwd[1].start()

        @pl.when(rb == 1)
        def _():
            load_refl.wait()
            v_sib.wait()
            v_fwd[0].wait()
            assemble(0)
            gram = dot(v_parts[col, 1], v_full[0], TN)
            gram = jnp.concatenate([gram[:, :half_panel], gram[:, half_panel:]], axis=0)
            g_buf[...] = gram.reshape(n_chunks, g_chunk, half_panel).astype(BF16)
            red_gram[0]()

        value = product(0, rb)
        for q in range(per_rb):
            make_mixing(1, rb * per_rb + q)
        on_send[0, rb] = value[:own].astype(BF16)
        on_copy(0, rb).start()
        hold[rb] = value[own:]

        @pl.when(rb > 0)
        def _():
            pass_across(rb - 1)

        return carry

    lax.fori_loop(0, n_rb, other_chip, 0)
    pass_across(n_rb - 1)

    my_rows = order_rows // n_chunks
    own_at = pl.ds(pl.multiple_of(col * own, LANES), own)
    own_sq, own_shift = asq_s[own_at, :], shift_s[own_at, :]
    squares = jnp.zeros((own, LANES), F32)
    for r in range(my_rows):
        at = pl.ds(row * my_rows + r, 1)
        sq_row = pole_ref[at, :]
        weight = jnp.where(side == 0, jnp.ones_like(sq_row), jnp.sqrt(sq_row))
        num_row = (1 - defl_ref[at, :]).astype(F32) * coup_ref[at, :] * weight
        secular = num_row / ((sq_row - own_sq) - own_shift)
        squares = squares + secular * secular
    sq_own[...] = jnp.zeros((8, LANES), F32)
    for h in range(own // LANES):
        column = jnp.sum(squares[h * LANES : (h + 1) * LANES, :], axis=1, keepdims=True)
        sq_own[h : h + 1, :] = jnp.broadcast_to(column, (LANES, LANES)).T[:1, :]
    sy_copies = [
        remote(sq_own, sq_y.at[d - 1], sy_ssem.at[d - 1], sy_rsem.at[d - 1], y_dev(d)) for d in range(1, n_y)
    ]
    sz_copies = [
        remote(sq_sum, sq_z.at[d - 1], sz_ssem.at[d - 1], sz_rsem.at[d - 1], z_dev(d)) for d in range(1, n_z)
    ]
    pl.semaphore_wait(meet_sem.at[1], len(middle))
    for copy in sy_copies:
        copy.start()
    red_gram[1]()

    def own_chip(rb, carry):
        value = product(1, rb)
        on_send[1, rb] = value[:own].astype(BF16)
        on_copy(1, rb).start()
        merged[rb] = value[own:]
        return carry

    lax.fori_loop(0, n_rb, own_chip, 0)
    v_fwd[1].wait()
    assemble(1)
    red_gram[3](red_gram[2]().astype(BF16))

    for rb in range(n_rb):
        at = slice(rb * R_TILE, (rb + 1) * R_TILE)
        on_copy(1, rb).wait()
        cr_copy(rb).wait()
        value = merged[rb] + on_recv[1, rb].astype(F32) + cr_recv[rb].astype(F32)
        merged[rb] = value
        value_low = value.astype(BF16)
        if rb < n_rb - 1:
            for p in range(2):
                term = dot(value_low, v_full[p, at, :], NN)
                proj_acc[p] = term if rb == 0 else proj_acc[p] + term
    for i in range(2):
        p = 1 - i
        term = proj_acc[p] + dot(value_low, v_full[p, at, :], NN)
        p_buf[i] = term.reshape(n_chunks, chunk, panel).astype(BF16)
        red_proj[i][0]()

    load_tri.wait()
    upper = lax.broadcasted_iota(jnp.int32, (panel, panel), 0) <= lax.broadcasted_iota(jnp.int32, (panel, panel), 1)
    for p in range(n_panels):
        u = jnp.where(upper, tri_v[p], 0.0)
        u_high = u.astype(BF16)
        u_hi[p] = u_high
        u_lo[p] = (u - u_high.astype(F32)).astype(BF16)

    for copy in sy_copies:
        copy.wait()
    total = sq_own[...]
    for d in range(1, n_y):
        total = total + sq_y[d - 1]
    sq_sum[...] = total
    for copy in sz_copies:
        copy.start()

    red_gram[4]()
    diagonal = {"col": (1 - x) * 2 + 1 - core}
    gram_copies = [
        remote(g_all, gram_all.at[col], gram_ssem.at[i], gram_rsem.at[i], peer)
        for i, peer in enumerate((across, diagonal, sib))
    ]
    for copy in gram_copies:
        copy.start()
    gram_all[col] = g_all[...]
    red_proj[0][1]()
    red_proj[1][1]()

    def apply_triangle(value, p):
        high = value.astype(BF16).astype(F32)
        stacked = jnp.concatenate([high, value - high], axis=0).astype(BF16)
        by_hi = dot(stacked, u_hi[p], NT)
        by_lo = dot(stacked, u_lo[p], NT)
        return (by_hi[:chunk] + (by_hi[chunk:] + by_lo[:chunk])).astype(BF16)

    coef_1 = apply_triangle(red_proj[0][2](), 1)
    red_proj[0][3](coef_1)
    gram_rows = []
    for copy in gram_copies:
        copy.wait()
    for c in range(n_col):
        quarter = gram_all[c].astype(F32).reshape(2 * blk, half_panel)
        gram_rows.append(jnp.concatenate([quarter[:blk], quarter[blk:]], axis=1))
    gram_rows = jnp.concatenate(gram_rows, axis=0).astype(BF16)
    carried = dot(coef_1, gram_rows, NN)
    coef_0 = apply_triangle(red_proj[1][2]() - carried, 0)
    red_proj[1][3](coef_0)
    for copy in sz_copies:
        copy.wait()
    total = sq_sum[...]
    for d in range(1, n_z):
        total = total + sq_z[d - 1]
    for h in range(own // LANES):
        scale = 1.0 / jnp.sqrt(as_column(total[h : h + 1, :]) + 1e-6)
        at = pl.ds(pl.multiple_of(col * own + h * LANES, LANES), LANES)
        scale_s[h * LANES : (h + 1) * LANES, :] = jnp.where(code_s[at, :] > -dead_mark, 1.0, scale)

    for i in range(2):
        p = 1 - i
        red_proj[i][4]()
        coef_all = p_all[i].astype(F32).reshape(own, panel).astype(BF16)
        for rb in range(n_rb):
            at = slice(rb * R_TILE, (rb + 1) * R_TILE)
            value = merged[rb] - dot(coef_all, v_full[p, at, :], NT)
            if i == 1:
                out_ref[0, :, at] = (value * jnp.tile(scale_s[...], (1, R_TILE // LANES))).astype(BF16)
            else:
                merged[rb] = value


def per_device(cfg, old_vectors, reflectors, triangles, pole_sq, coupling, deflated, pole_order, anchors, root_fraction):
    n_y, n_z, n_col, triplets, width, rows, n_panels, order_rows, panel = cfg
    own = triplets // n_col
    n_rb = rows // R_TILE
    chunk = own // (n_y * n_z)
    lane_rows = lambda a: a.reshape(-1, LANES)
    dma, vmem = pltpu.SemaphoreType.DMA, pltpu.VMEM
    n_row, half = n_y * n_z, panel // 2
    g_chunk = 2 * (panel // n_col) // n_row
    scratch = [
        vmem((rows, width), BF16),
        vmem((n_panels, panel, panel), F32),
        vmem((n_col, n_panels, rows, panel // n_col), BF16),
        vmem((n_panels, rows, panel), BF16),
        vmem((n_panels, panel, panel), BF16),
        vmem((n_panels, panel, panel), BF16),
        vmem((order_rows, 9 * LANES), BF16),
        vmem((8, width), F32),
        vmem((8, width), F32),
        vmem((triplets, LANES), F32),
        vmem((triplets, LANES), F32),
        vmem((triplets, LANES), F32),
        vmem((own, LANES), F32),
        vmem((2, 2 * own, width), BF16),
        vmem((n_rb, own, R_TILE), F32),
        vmem((n_rb, own, R_TILE), F32),
        vmem((2, own, panel), F32),
        vmem((2, n_rb, own, R_TILE), BF16),
        vmem((2, n_rb, own, R_TILE), BF16),
        vmem((n_rb, own, R_TILE), BF16),
        vmem((n_rb, own, R_TILE), BF16),
        vmem((n_col, n_row, g_chunk, half), BF16),
        vmem((8, LANES), F32), vmem((n_y - 1, 8, LANES), F32),
        vmem((8, LANES), F32), vmem((n_z - 1, 8, LANES), F32),
        vmem((2, n_row, chunk, panel), BF16),
        vmem((2, n_y - 1, n_z, chunk, panel), BF16),
        vmem((2, n_z, chunk, panel), BF16),
        vmem((2, n_z - 1, chunk, panel), BF16),
        vmem((2, n_row, chunk, panel), BF16),
        vmem((n_row, g_chunk, half), BF16),
        vmem((n_y - 1, n_z, g_chunk, half), BF16),
        vmem((n_z, g_chunk, half), BF16),
        vmem((n_z - 1, g_chunk, half), BF16),
        vmem((n_row, g_chunk, half), BF16),
        dma((3,)), dma((5,)), dma((5,)),
        dma((2, n_rb)), dma((2, n_rb)), dma((n_rb,)), dma((n_rb,)), dma((3,)), dma((3,)),
        dma((n_y - 1,)), dma((n_y - 1,)), dma((n_z - 1,)), dma((n_z - 1,)),
        dma((3, n_y - 1)), dma((3, n_y - 1)),
        dma((3, n_z - 1)), dma((3, n_z - 1)),
        dma((3, n_row - 1)), dma((3, n_row - 1)), pltpu.SemaphoreType.REGULAR((2,)),
    ]
    any_spec, vmem_spec = pl.BlockSpec(memory_space=pl.ANY), pl.BlockSpec(memory_space=pltpu.VMEM)
    return pl.pallas_call(
        functools.partial(kernel, cfg),
        out_shape=jax.ShapeDtypeStruct((1, own, rows), BF16),
        in_specs=[any_spec] * 3 + [vmem_spec] * 6,
        out_specs=vmem_spec,
        scratch_shapes=scratch,
        compiler_params=pltpu.CompilerParams(
            collective_id=0, has_side_effects=True, vmem_limit_bytes=56 << 20
        ),
    )(
        old_vectors, reflectors, triangles,
        lane_rows(pole_sq), lane_rows(coupling), lane_rows(deflated), lane_rows(pole_order),
        lane_rows(anchors), lane_rows(root_fraction),
    )


def solution(mesh):
    n_row, n_col = mesh.shape["row"], mesh.shape["col"]
    n_y = 4
    n_z = n_row // n_y

    def whole(old_vectors, reflectors, triangles, pole_sq, coupling, deflated, pole_order, anchors, root_fraction):
        size, panel = reflectors.shape[2:]
        cfg = (
            n_y, n_z, n_col, anchors.shape[0], old_vectors.shape[2] // n_col, size // n_row,
            reflectors.shape[1], size // LANES, panel,
        )
        in_specs = (P("side", "row", "col"), P("side", None, "row", "col"), P("side", None, None, None)) + (P(),) * 6
        return jax.shard_map(
            functools.partial(per_device, cfg), mesh=mesh, in_specs=in_specs,
            out_specs=P("side", "col", "row"), check_vma=False,
        )(old_vectors, reflectors, triangles, pole_sq, coupling, deflated, pole_order, anchors, root_fraction)

    return whole
```

```python
import functools

import jax
import jax.numpy as jnp
from jax import lax
from jax.experimental import pallas as pl
from jax.experimental.pallas import tpu as pltpu
from jax.sharding import PartitionSpec as P

LANES = 128
R_TILE = 256
PIECES = 3
F32 = jnp.float32
BF16 = jnp.bfloat16
MESH = pl.DeviceIdType.MESH
NT = (((1,), (1,)), ((), ()))
NN = (((1,), (0,)), ((), ()))
TN = (((0,), (0,)), ((), ()))


def dot(lhs, rhs, dims):
    return lax.dot_general(lhs, rhs, dims, preferred_element_type=F32)


def split3(value):
    high = value.astype(BF16).astype(F32)
    rest = value - high
    middle = rest.astype(BF16).astype(F32)
    return high, middle, rest - middle


def as_column(row):
    return jnp.broadcast_to(row.astype(F32), (LANES, LANES)).T


def kernel(
    cfg,
    old_hbm, refl_hbm, tri_hbm, pole_ref, coup_ref, defl_ref, order_ref, anchor_ref, frac_ref,
    out_ref,
    old_v, tri_v, v_parts, v_full, u_hi, u_lo, table, col_sq, col_num, asq_s, shift_s, code_s, scale_s,
    mix, hold, merged, proj_acc, on_send, on_recv, cr_send, cr_recv, gram_all,
    sq_own, sq_y, sq_sum, sq_z,
    p_buf, p_y, p_z, p_zr, p_all, g_buf, g_y, g_z, g_zr, g_all,
    load_sem, v_send, v_recv, on_ssem, on_rsem, cr_ssem, cr_rsem, gram_ssem, gram_rsem,
    sy_ssem, sy_rsem, sz_ssem, sz_rsem,
    ys_sem, yr_sem, zs_sem, zr_sem, b_ssem, b_rsem, meet_sem,
):
    n_y, n_z, n_col, triplets, width, rows, n_panels, order_rows, panel = cfg
    own = triplets // n_col
    half_rows = n_y * n_z // 2
    n_chunks = n_y * n_z
    n_hi = width // LANES
    n_rb = rows // R_TILE
    chunk = own // n_chunks
    blk = panel // n_col
    half_panel = panel // 2
    g_chunk = 2 * blk // n_chunks
    scatter_rows = order_rows // 2

    side = lax.axis_index("side")
    row = lax.axis_index("row")
    col = lax.axis_index("col")
    y, z = row // n_z, row % n_z
    x, core = col // 2, col % 2
    sib = {"col": x * 2 + 1 - core}
    across = {"col": (1 - x) * 2 + core}

    def y_peer(d):
        return lax.rem(y + d, n_y)

    def z_peer(d):
        return lax.rem(z + d, n_z)

    def y_dev(d):
        return {"row": y_peer(d) * n_z + z}

    def z_dev(d):
        return {"row": y * n_z + z_peer(d)}

    y_near = sorted({1, n_y - 1})
    z_near = sorted({1, n_z - 1})
    z_mid = sorted({d % n_z for d in (1, -1, 2, -2)} - {0})
    near = [y_dev(d) for d in y_near] + [z_dev(d) for d in z_near]
    middle = [z_dev(d) for d in z_mid]
    peers = [sib, across] + near
    barrier = pltpu.get_barrier_semaphore()
    for peer in peers:
        pl.semaphore_signal(barrier, inc=1, device_id=peer, device_id_type=MESH)

    load_refl = pltpu.make_async_copy(refl_hbm.at[0], v_parts.at[col], load_sem.at[1])
    load_old = pltpu.make_async_copy(old_hbm.at[0], old_v, load_sem.at[0])
    load_tri = pltpu.make_async_copy(tri_hbm.at[0], tri_v, load_sem.at[2])
    load_refl.start()
    load_old.start()

    def remote(src, dst, ssem, rsem, peer):
        return pltpu.make_async_remote_copy(
            src_ref=src, dst_ref=dst, send_sem=ssem, recv_sem=rsem, device_id=peer, device_id_type=MESH
        )

    first = row // half_rows * (width * n_col) + col * width
    sub_hi = lax.broadcasted_iota(jnp.int32, (n_hi, LANES), 0)
    sub_lo = lax.broadcasted_iota(jnp.int32, (LANES, LANES), 0)

    def scatter(g, acc):
        left, right = [], []
        for b in range(scatter_rows // 8):
            at = pl.ds(pl.multiple_of(g * scatter_rows + b * 8, 8), 8)
            place = order_ref[at, :] - first
            hi, lo = place >> 7, place & (LANES - 1)
            live = (1 - defl_ref[at, :]).astype(F32) * coup_ref[at, :]
            values = split3(pole_ref[at, :]) + split3(live)
            for r in range(8):
                mask = hi[r : r + 1, :] == sub_hi
                left.append(
                    jnp.concatenate([jnp.where(mask, v[r : r + 1, :], 0.0) for v in values], axis=0).astype(BF16)
                )
                right.append(jnp.where(lo[r : r + 1, :] == sub_lo, 1.0, 0.0).astype(BF16))
        return acc + dot(jnp.concatenate(left, axis=1), jnp.concatenate(right, axis=1), NT)

    placed = scatter(0, jnp.zeros((2 * PIECES * n_hi, LANES), F32))

    pl.semaphore_wait(barrier, len(peers))
    for peer in near:
        pl.semaphore_signal(meet_sem.at[0], inc=1, device_id=peer, device_id_type=MESH)

    v_fwd_at = (1 - x) * 2 + core
    v_across, v_fwd = [], []
    for p in range(2):
        v_across.append(remote(refl_hbm.at[0, p], v_parts.at[col, p], v_send.at[p], v_recv.at[p], across))
        v_fwd.append(
            remote(v_parts.at[v_fwd_at, p], v_parts.at[v_fwd_at, p], v_send.at[2 + p], v_recv.at[2 + p], sib)
        )
    v_sib = remote(refl_hbm.at[0], v_parts.at[col], v_send.at[4], v_recv.at[4], sib)
    v_across[0].start()
    v_sib.start()
    load_tri.start()

    placed = scatter(1, placed)
    part = [placed[i * n_hi : (i + 1) * n_hi, :] for i in range(2 * PIECES)]
    sq = (part[0] + part[1]) + part[2]
    num = (part[3] + part[4]) + part[5]
    num = num * jnp.where(side == 0, jnp.ones_like(sq), jnp.sqrt(sq))
    for h in range(n_hi):
        lanes = slice(h * LANES, (h + 1) * LANES)
        col_sq[:, lanes] = jnp.broadcast_to(sq[h : h + 1, :], (8, LANES))
        col_num[:, lanes] = jnp.broadcast_to(num[h : h + 1, :], (8, LANES))

    pole = pole_ref[...]
    ahead = pltpu.roll(pole, LANES - 1, 1)
    wrapped = pltpu.roll(ahead, order_rows - 1, 0)
    lane_all = lax.broadcasted_iota(jnp.int32, (order_rows, LANES), 1)
    after = jnp.where(lane_all == LANES - 1, wrapped, ahead)
    order = order_ref[...]
    entries = split3(pole) + split3(after) + (
        (order >> 7).astype(F32), (order & (LANES - 1)).astype(F32), defl_ref[...].astype(F32),
    )
    for i, entry in enumerate(entries):
        table[:, i * LANES : (i + 1) * LANES] = entry.astype(BF16)
    lane_row = lax.broadcasted_iota(jnp.int32, (LANES, LANES), 1)
    lane_table = lax.broadcasted_iota(jnp.int32, (LANES, order_rows), 1)
    dead_mark = 65536.0

    for jb in range(triplets // LANES):
        anchor = as_column(anchor_ref[jb : jb + 1, :]).astype(jnp.int32)
        frac = as_column(frac_ref[jb : jb + 1, :])
        pick_hi = jnp.where((anchor >> 7)[:, :1] == lane_table, 1.0, 0.0).astype(BF16)
        found = dot(pick_hi, table[...], NN)
        f = [found[:, i * LANES : (i + 1) * LANES] for i in range(9)]
        pick_lo = (anchor & (LANES - 1)) == lane_row

        def chosen(value):
            return jnp.sum(jnp.where(pick_lo, value, 0.0), axis=1, keepdims=True)

        a_sq = chosen((f[0] + f[1]) + f[2])
        a_next = chosen((f[3] + f[4]) + f[5])
        target = chosen((f[6] * float(LANES) + f[7]) + f[8] * dead_mark)
        gap = a_next - a_sq
        code = jnp.where(target >= dead_mark, target - dead_mark - first.astype(F32), -dead_mark)
        at = slice(jb * LANES, (jb + 1) * LANES)
        asq_s[at, :] = jnp.broadcast_to(a_sq, (LANES, LANES))
        shift_s[at, :] = frac * gap
        code_s[at, :] = jnp.broadcast_to(code, (LANES, LANES))

    v_across[1].start()
    pl.semaphore_wait(meet_sem.at[0], len(near))
    for peer in middle:
        pl.semaphore_signal(meet_sem.at[1], inc=1, device_id=peer, device_id_type=MESH)

    lane_wide = lax.broadcasted_iota(jnp.int32, (8, width), 1).astype(F32)

    def make_mixing(grp, g):
        chip = 1 - x if grp == 0 else x
        base = jnp.where(g < own // 16, (chip * 2 + 1 - core) * own, (chip * 2 + core) * own - own)
        parts = []
        for half in range(2):
            at = pl.ds(pl.multiple_of(base + g * 16 + half * 8, 8), 8)
            a_sq = jnp.tile(asq_s[at, :], (1, n_hi))
            shift = jnp.tile(shift_s[at, :], (1, n_hi))
            code = jnp.tile(code_s[at, :], (1, n_hi))
            den = (col_sq[...] - a_sq) - shift
            value = col_num[...] / den
            onehot = jnp.where(lane_wide == code, 1.0, 0.0)
            parts.append(jnp.where(code > -dead_mark, onehot, value))
        mix[grp, pl.ds(pl.multiple_of(g * 16, 16), 16), :] = jnp.concatenate(parts, axis=0).astype(BF16)

    def first_mixing(g, carry):
        make_mixing(0, g)
        return carry

    lax.fori_loop(0, own // 8, first_mixing, 0)
    load_old.wait()

    def product(grp, rb):
        return dot(mix[grp], old_v[pl.ds(pl.multiple_of(rb * R_TILE, R_TILE), R_TILE), :], NT)

    def on_copy(grp, rb):
        return remote(
            on_send.at[grp, rb], on_recv.at[grp, rb], on_ssem.at[grp, rb], on_rsem.at[grp, rb], sib
        )

    def cr_copy(rb):
        return remote(cr_send.at[rb], cr_recv.at[rb], cr_ssem.at[rb], cr_rsem.at[rb], across)

    def pass_across(rb):
        on_copy(0, rb).wait()
        cr_send[rb] = (hold[rb] + on_recv[0, rb].astype(F32)).astype(BF16)
        cr_copy(rb).start()

    far = [(dy, dz) for dy in range(n_y) for dz in range(n_z) if dy or dz]
    far.sort(key=lambda d: -(min(d[0], n_y - d[0]) + min(d[1], n_z - d[1])))

    def far_dev(dy, dz):
        return {"row": y_peer(dy) * n_z + z_peer(dz)}

    def reduction(i, buf, from_y, z_in, from_z, everything):
        y_out = [
            remote(buf.at[pl.ds(y_peer(d) * n_z, n_z)], from_y.at[d - 1], ys_sem.at[i, d - 1], yr_sem.at[i, d - 1], y_dev(d))
            for d in sorted(range(1, n_y), key=lambda d: -min(d, n_y - d))
        ]
        z_out = [
            remote(z_in.at[z_peer(d)], from_z.at[d - 1], zs_sem.at[i, d - 1], zr_sem.at[i, d - 1], z_dev(d))
            for d in sorted(range(1, n_z), key=lambda d: -min(d, n_z - d))
        ]
        mine = everything.at[row]
        back = [remote(mine, mine, b_ssem.at[i, k], b_rsem.at[i, k], far_dev(dy, dz)) for k, (dy, dz) in enumerate(far)]

        def start(copies):
            for copy in copies:
                copy.start()

        def wait(copies):
            for copy in copies:
                copy.wait()

        def y_to_z():
            wait(y_out)
            summed = buf[pl.ds(y * n_z, n_z)].astype(F32)
            for d in range(1, n_y):
                summed = summed + from_y[d - 1].astype(F32)
            z_in[...] = summed.astype(BF16)
            start(z_out)

        def finish():
            wait(z_out)
            summed = z_in[z].astype(F32)
            for d in range(1, n_z):
                summed = summed + from_z[d - 1].astype(F32)
            return summed

        def send_back(value):
            everything[row] = value
            start(back)

        return (lambda: start(y_out)), y_to_z, finish, send_back, (lambda: wait(back))

    red_proj = [
        reduction(i, p_buf.at[i], p_y.at[i], p_z.at[i], p_zr.at[i], p_all.at[i]) for i in range(2)
    ]
    red_gram = reduction(2, g_buf, g_y, g_z, g_zr, g_all)

    per_rb = own // 8 // n_rb

    def assemble(p):
        for c in range(n_col):
            v_full[p, :, c * blk : (c + 1) * blk] = v_parts[c, p]

    v_across[0].wait()
    v_fwd[0].start()

    def other_chip(rb, carry):
        @pl.when(rb == n_rb - 1)
        def _():
            v_across[1].wait()
            v_fwd[1].start()

        @pl.when(rb == 1)
        def _():
            load_refl.wait()
            v_sib.wait()
            v_fwd[0].wait()
            assemble(0)
            gram = dot(v_parts[col, 1], v_full[0], TN)
            gram = jnp.concatenate([gram[:, :half_panel], gram[:, half_panel:]], axis=0)
            g_buf[...] = gram.reshape(n_chunks, g_chunk, half_panel).astype(BF16)
            red_gram[0]()

        value = product(0, rb)
        for q in range(per_rb):
            make_mixing(1, rb * per_rb + q)
        on_send[0, rb] = value[:own].astype(BF16)
        on_copy(0, rb).start()
        hold[rb] = value[own:]

        @pl.when(rb > 0)
        def _():
            pass_across(rb - 1)

        return carry

    lax.fori_loop(0, n_rb, other_chip, 0)
    pass_across(n_rb - 1)

    my_rows = order_rows // n_chunks
    own_at = pl.ds(pl.multiple_of(col * own, LANES), own)
    own_sq, own_shift = asq_s[own_at, :], shift_s[own_at, :]
    squares = jnp.zeros((own, LANES), F32)
    for r in range(my_rows):
        at = pl.ds(row * my_rows + r, 1)
        sq_row = pole_ref[at, :]
        weight = jnp.where(side == 0, jnp.ones_like(sq_row), jnp.sqrt(sq_row))
        num_row = (1 - defl_ref[at, :]).astype(F32) * coup_ref[at, :] * weight
        secular = num_row / ((sq_row - own_sq) - own_shift)
        squares = squares + secular * secular
    sq_own[...] = jnp.zeros((8, LANES), F32)
    for h in range(own // LANES):
        column = jnp.sum(squares[h * LANES : (h + 1) * LANES, :], axis=1, keepdims=True)
        sq_own[h : h + 1, :] = jnp.broadcast_to(column, (LANES, LANES)).T[:1, :]
    sy_copies = [
        remote(sq_own, sq_y.at[d - 1], sy_ssem.at[d - 1], sy_rsem.at[d - 1], y_dev(d)) for d in range(1, n_y)
    ]
    sz_copies = [
        remote(sq_sum, sq_z.at[d - 1], sz_ssem.at[d - 1], sz_rsem.at[d - 1], z_dev(d)) for d in range(1, n_z)
    ]
    pl.semaphore_wait(meet_sem.at[1], len(middle))
    for copy in sy_copies:
        copy.start()
    red_gram[1]()

    def own_chip(rb, carry):
        value = product(1, rb)
        on_send[1, rb] = value[:own].astype(BF16)
        on_copy(1, rb).start()
        merged[rb] = value[own:]
        return carry

    lax.fori_loop(0, n_rb, own_chip, 0)
    v_fwd[1].wait()
    assemble(1)
    red_gram[3](red_gram[2]().astype(BF16))

    for rb in range(n_rb):
        at = slice(rb * R_TILE, (rb + 1) * R_TILE)
        on_copy(1, rb).wait()
        cr_copy(rb).wait()
        value = merged[rb] + on_recv[1, rb].astype(F32) + cr_recv[rb].astype(F32)
        merged[rb] = value
        value_low = value.astype(BF16)
        if rb < n_rb - 1:
            for p in range(2):
                term = dot(value_low, v_full[p, at, :], NN)
                proj_acc[p] = term if rb == 0 else proj_acc[p] + term
    for i in range(2):
        p = 1 - i
        term = proj_acc[p] + dot(value_low, v_full[p, at, :], NN)
        p_buf[i] = term.reshape(n_chunks, chunk, panel).astype(BF16)
        red_proj[i][0]()

    load_tri.wait()
    upper = lax.broadcasted_iota(jnp.int32, (panel, panel), 0) <= lax.broadcasted_iota(jnp.int32, (panel, panel), 1)
    for p in range(n_panels):
        u = jnp.where(upper, tri_v[p], 0.0)
        u_high = u.astype(BF16)
        u_hi[p] = u_high
        u_lo[p] = (u - u_high.astype(F32)).astype(BF16)

    for copy in sy_copies:
        copy.wait()
    total = sq_own[...]
    for d in range(1, n_y):
        total = total + sq_y[d - 1]
    sq_sum[...] = total
    for copy in sz_copies:
        copy.start()

    red_gram[4]()
    diagonal = {"col": (1 - x) * 2 + 1 - core}
    gram_copies = [
        remote(g_all, gram_all.at[col], gram_ssem.at[i], gram_rsem.at[i], peer)
        for i, peer in enumerate((across, diagonal, sib))
    ]
    for copy in gram_copies:
        copy.start()
    gram_all[col] = g_all[...]
    red_proj[0][1]()
    red_proj[1][1]()

    def apply_triangle(value, p):
        high = value.astype(BF16).astype(F32)
        stacked = jnp.concatenate([high, value - high], axis=0).astype(BF16)
        by_hi = dot(stacked, u_hi[p], NT)
        by_lo = dot(stacked, u_lo[p], NT)
        return (by_hi[:chunk] + (by_hi[chunk:] + by_lo[:chunk])).astype(BF16)

    coef_1 = apply_triangle(red_proj[0][2](), 1)
    red_proj[0][3](coef_1)
    gram_rows = []
    for copy in gram_copies:
        copy.wait()
    for c in range(n_col):
        quarter = gram_all[c].astype(F32).reshape(2 * blk, half_panel)
        gram_rows.append(jnp.concatenate([quarter[:blk], quarter[blk:]], axis=1))
    gram_rows = jnp.concatenate(gram_rows, axis=0).astype(BF16)
    carried = dot(coef_1, gram_rows, NN)
    coef_0 = apply_triangle(red_proj[1][2]() - carried, 0)
    red_proj[1][3](coef_0)
    for copy in sz_copies:
        copy.wait()
    total = sq_sum[...]
    for d in range(1, n_z):
        total = total + sq_z[d - 1]
    for h in range(own // LANES):
        scale = 1.0 / jnp.sqrt(as_column(total[h : h + 1, :]) + 1e-6)
        at = pl.ds(pl.multiple_of(col * own + h * LANES, LANES), LANES)
        scale_s[h * LANES : (h + 1) * LANES, :] = jnp.where(code_s[at, :] > -dead_mark, 1.0, scale)

    for i in range(2):
        p = 1 - i
        red_proj[i][4]()
        coef_all = p_all[i].astype(F32).reshape(own, panel).astype(BF16)
        for rb in range(n_rb):
            at = slice(rb * R_TILE, (rb + 1) * R_TILE)
            value = merged[rb] - dot(coef_all, v_full[p, at, :], NT)
            if i == 1:
                out_ref[0, :, at] = (value * jnp.tile(scale_s[...], (1, R_TILE // LANES))).astype(BF16)
            else:
                merged[rb] = value


def per_device(cfg, old_vectors, reflectors, triangles, pole_sq, coupling, deflated, pole_order, anchors, root_fraction):
    n_y, n_z, n_col, triplets, width, rows, n_panels, order_rows, panel = cfg
    own = triplets // n_col
    n_rb = rows // R_TILE
    chunk = own // (n_y * n_z)
    lane_rows = lambda a: a.reshape(-1, LANES)
    dma, vmem = pltpu.SemaphoreType.DMA, pltpu.VMEM
    n_row, half = n_y * n_z, panel // 2
    g_chunk = 2 * (panel // n_col) // n_row
    scratch = [
        vmem((rows, width), BF16),
        vmem((n_panels, panel, panel), F32),
        vmem((n_col, n_panels, rows, panel // n_col), BF16),
        vmem((n_panels, rows, panel), BF16),
        vmem((n_panels, panel, panel), BF16),
        vmem((n_panels, panel, panel), BF16),
        vmem((order_rows, 9 * LANES), BF16),
        vmem((8, width), F32),
        vmem((8, width), F32),
        vmem((triplets, LANES), F32),
        vmem((triplets, LANES), F32),
        vmem((triplets, LANES), F32),
        vmem((own, LANES), F32),
        vmem((2, 2 * own, width), BF16),
        vmem((n_rb, own, R_TILE), F32),
        vmem((n_rb, own, R_TILE), F32),
        vmem((2, own, panel), F32),
        vmem((2, n_rb, own, R_TILE), BF16),
        vmem((2, n_rb, own, R_TILE), BF16),
        vmem((n_rb, own, R_TILE), BF16),
        vmem((n_rb, own, R_TILE), BF16),
        vmem((n_col, n_row, g_chunk, half), BF16),
        vmem((8, LANES), F32), vmem((n_y - 1, 8, LANES), F32),
        vmem((8, LANES), F32), vmem((n_z - 1, 8, LANES), F32),
        vmem((2, n_row, chunk, panel), BF16),
        vmem((2, n_y - 1, n_z, chunk, panel), BF16),
        vmem((2, n_z, chunk, panel), BF16),
        vmem((2, n_z - 1, chunk, panel), BF16),
        vmem((2, n_row, chunk, panel), BF16),
        vmem((n_row, g_chunk, half), BF16),
        vmem((n_y - 1, n_z, g_chunk, half), BF16),
        vmem((n_z, g_chunk, half), BF16),
        vmem((n_z - 1, g_chunk, half), BF16),
        vmem((n_row, g_chunk, half), BF16),
        dma((3,)), dma((5,)), dma((5,)),
        dma((2, n_rb)), dma((2, n_rb)), dma((n_rb,)), dma((n_rb,)), dma((3,)), dma((3,)),
        dma((n_y - 1,)), dma((n_y - 1,)), dma((n_z - 1,)), dma((n_z - 1,)),
        dma((3, n_y - 1)), dma((3, n_y - 1)),
        dma((3, n_z - 1)), dma((3, n_z - 1)),
        dma((3, n_row - 1)), dma((3, n_row - 1)), pltpu.SemaphoreType.REGULAR((2,)),
    ]
    any_spec, vmem_spec = pl.BlockSpec(memory_space=pl.ANY), pl.BlockSpec(memory_space=pltpu.VMEM)
    return pl.pallas_call(
        functools.partial(kernel, cfg),
        out_shape=jax.ShapeDtypeStruct((1, own, rows), BF16),
        in_specs=[any_spec] * 3 + [vmem_spec] * 6,
        out_specs=vmem_spec,
        scratch_shapes=scratch,
        compiler_params=pltpu.CompilerParams(
            collective_id=0, has_side_effects=True, vmem_limit_bytes=56 << 20
        ),
    )(
        old_vectors, reflectors, triangles,
        lane_rows(pole_sq), lane_rows(coupling), lane_rows(deflated), lane_rows(pole_order),
        lane_rows(anchors), lane_rows(root_fraction),
    )


def solution(mesh):
    n_row, n_col = mesh.shape["row"], mesh.shape["col"]
    n_y = 4
    n_z = n_row // n_y

    def whole(old_vectors, reflectors, triangles, pole_sq, coupling, deflated, pole_order, anchors, root_fraction):
        size, panel = reflectors.shape[2:]
        cfg = (
            n_y, n_z, n_col, anchors.shape[0], old_vectors.shape[2] // n_col, size // n_row,
            reflectors.shape[1], size // LANES, panel,
        )
        in_specs = (P("side", "row", "col"), P("side", None, "row", "col"), P("side", None, None, None)) + (P(),) * 6
        return jax.shard_map(
            functools.partial(per_device, cfg), mesh=mesh, in_specs=in_specs,
            out_specs=P("side", "col", "row"), check_vma=False,
        )(old_vectors, reflectors, triangles, pole_sq, coupling, deflated, pole_order, anchors, root_fraction)

    return whole
```
